32 devices in a mesh: src: 8 (over z, x), tgt: 4 (over y, core).
Axes of the slice: x: 2, y: 2, z: 4, core: 2. Of those that a mesh axis runs over, the one named last changes fastest.
Arguments:
- source_points: bfloat16 [65536, 128], P('src'), may hold values from -1.796875 to 1.796875
- target_points: bfloat16 [196608, 128], P('tgt'), may hold values from -1.796875 to 1.796875
- source_potential: float32 [65536], P('src'), may hold values from -6 to 122
- target_potential: float32 [196608], P('tgt'), may hold values from -6 to 122
- source_log_mass: float32 [65536], P('src'), may hold values from -1.5 to 1.5
- target_log_mass: float32 [196608], P('tgt'), may hold values from -1.5 to 1.5
- pair_targets: int32 [64, 10], P('src'), may hold values from 0 to 191, as said below
- pair_counts: int32 [64], P('src'), may hold values from 4 to 10, as said below
Outputs:
- row_potential: float32 [65536], P('src')
- column_potential: float32 [196608], P('tgt')
The draws below stay inside these ranges and needn't reach their ends.
Inputs may be any that keep to these rules, and one draw needn't show every extreme that they name: For k < pair_counts[b], pair_targets[b, k] are distinct target blocks paired with source block b; the later entries of a row are target block numbers too but name no pair; every target block is named by some pair. `pair_counts`: some source block has exactly 10 pairs.
All inputs are finite; a program needn't handle non-finite values.
Results may differ from the reference program's by a relative error of at most 0.0003.
Values may be sent and summed in bfloat16 or wider, within the bound.
No kernel may reach another device: no remote copies, remote signals or barrier semaphores. Data moves between devices by JAX's collectives and lax.ppermute only.
A program may use at most 128 MiB of HBM per device.

```python
import jax
import jax.numpy as jnp
from jax import lax

D = 128
BLK = 1024
K = 10
ITERS = 2
SB_DEV = 8
TB_DEV = 48
NSB = 64
NTB = 192
NS = 65536
NT = 196608


def pair_layout(key):
    base = jax.random.fold_in(key, 4242)
    keys = jax.random.split(base, 6)
    source_groups = NSB // SB_DEV
    target_groups = NTB // TB_DEV
    lowest = max(4, (NTB + NSB - 1) // NSB)
    counts = jax.random.randint(keys[0], (NSB,), lowest, K + 1)
    fullest = jax.random.randint(keys[1], (), 0, NSB)
    counts = jnp.where(jnp.arange(NSB) == fullest, K, counts).astype(jnp.int32)
    favored = jax.random.randint(keys[2], (source_groups,), 0, target_groups)
    coins = jax.random.randint(keys[3], (NSB,), 0, 2)
    wander = jax.random.randint(keys[4], (NSB,), 0, target_groups)
    homes = jnp.where(coins == 0, wander, favored[jnp.arange(NSB) // SB_DEV])
    blocks = jnp.arange(NTB, dtype=jnp.int32)
    forced = blocks[None, :] % NSB == jnp.arange(NSB, dtype=jnp.int32)[:, None]
    distant = blocks[None, :] // TB_DEV != homes[:, None]
    noise = jax.random.randint(keys[5], (NSB, NTB), 0, NTB)
    bucket = jnp.where(forced, 0, jnp.where(distant, 2, 1))
    ranking = (bucket * NTB + noise) * NTB + blocks[None, :]
    chosen = jnp.argsort(ranking, axis=1)[:, :K]
    return (chosen.astype(jnp.int32), counts)


def draw_pair_targets(key, part):
    return pair_layout(key)[0]


def draw_pair_counts(key, part):
    return pair_layout(key)[1]


def potential_draw(key, length, salt):
    keys = jax.random.split(jax.random.fold_in(key, salt), 1)
    return jnp.clip(jax.random.normal(keys[0], (length,), jnp.float32), -6.0, 6.0)


def draw_source_potential(key, part):
    return potential_draw(key, NS, 99)


def draw_target_potential(key, part):
    return potential_draw(key, NT, 177)


def block_scale(stream_key, shape, pieces, smallest, largest):
    gain = 1.0
    for axis_at, parts in pieces:
        draws = jax.random.uniform(jax.random.fold_in(jax.random.fold_in(stream_key, 6), axis_at), (parts,), jnp.float32, smallest / len(pieces), largest / len(pieces))
        gain = gain * jnp.repeat(jnp.exp(draws), shape[axis_at] // parts).reshape((-1,) + (1,) * (len(shape) - 1 - axis_at))
    return gain


def scatter_about(rng, shape, spread, bound, shards=(), held_as=jnp.bfloat16):
    result = spread * jax.random.normal(rng, shape, jnp.float32)
    if shards:
        result = result * block_scale(rng, shape, shards, -0.22, 0.18)
    return jnp.clip(result, -bound, bound).astype(held_as)


def setup_inputs(seed: int = 0) -> dict:
    splits = jax.random.split(jax.random.key(seed), 9)
    return {
        "source_points": scatter_about(splits[0], (NS, D), 0.3, 1.796875, ((0, 8),)),
        "target_points": scatter_about(splits[1], (NT, D), 0.3, 1.796875, ((0, 4),)),
        "source_potential": draw_source_potential(jax.random.fold_in(splits[8], 71), 0),
        "target_potential": draw_target_potential(jax.random.fold_in(splits[8], 71), 0),
        "source_log_mass": jnp.clip(jax.random.uniform(splits[4], (NS,), jnp.float32, -1.5, 1.5) * block_scale(splits[4], (NS,), ((0, 8),), -0.4, 0.0), -1.5, 1.5),
        "target_log_mass": jnp.clip(jax.random.uniform(splits[5], (NT,), jnp.float32, -1.5, 1.5) * block_scale(splits[5], (NT,), ((0, 4),), -0.4, 0.0), -1.5, 1.5),
        "pair_targets": draw_pair_targets(jax.random.fold_in(splits[8], 71), 0),
        "pair_counts": draw_pair_counts(jax.random.fold_in(splits[8], 71), 0),
    }


epsilon = 0.5
floor_max = -1.0e30


def half_squares(points):
    widened = points.astype(jnp.float32)
    return 0.5 * jnp.sum(widened * widened, axis=1)


def combine(first, second):
    highest = jnp.maximum(first[0], second[0])
    summed = first[1] * jnp.exp(first[0] - highest) + second[1] * jnp.exp(second[0] - highest)
    return (highest, summed)


def tile_stats(source_block, target_block, row_shift, column_shift):
    scaled = lax.dot_general(source_block, target_block, (((1,), (1,)), ((), ())), preferred_element_type=jnp.float32) / epsilon
    row_scores = scaled + column_shift[None, :]
    row_high = jnp.max(row_scores, axis=1)
    row_mass = jnp.sum(jnp.exp(row_scores - row_high[:, None]), axis=1)
    column_scores = scaled + row_shift[:, None]
    column_high = jnp.max(column_scores, axis=0)
    column_mass = jnp.sum(jnp.exp(column_scores - column_high[None, :]), axis=0)
    return (row_high, row_mass), (column_high, column_mass)


def updated(potential, log_mass, squares, highest, summed):
    fresh = epsilon * log_mass + squares - epsilon * (highest + jnp.log(summed))
    return 0.5 * (potential + fresh)


def reference(source_points, target_points, source_potential, target_potential, source_log_mass, target_log_mass, pair_targets, pair_counts):
    source_squares = half_squares(source_points)
    target_squares = half_squares(target_points)
    source_blocks = source_points.reshape(NSB, BLK, D)
    target_blocks = target_points.reshape(NTB, BLK, D)
    row_potential = source_potential
    column_potential = target_potential
    for sweep in range(ITERS):
        row_shift = ((row_potential - source_squares) / epsilon).reshape(NSB, BLK)
        column_shift = ((column_potential - target_squares) / epsilon).reshape(NTB, BLK)

        def per_block(columns, inputs):
            points, shift, targets, count = inputs

            def per_slot(state, position):
                def live(current):
                    row_high, row_mass, column_high, column_mass = current
                    target = targets[position]
                    other = lax.dynamic_index_in_dim(target_blocks, target, 0, keepdims=False)
                    other_shift = lax.dynamic_index_in_dim(column_shift, target, 0, keepdims=False)
                    row_part, column_part = tile_stats(points, other, shift, other_shift)
                    row_high, row_mass = combine((row_high, row_mass), row_part)
                    before = (lax.dynamic_index_in_dim(column_high, target, 0, keepdims=False), lax.dynamic_index_in_dim(column_mass, target, 0, keepdims=False))
                    after = combine(before, column_part)
                    column_high = lax.dynamic_update_index_in_dim(column_high, after[0], target, 0)
                    column_mass = lax.dynamic_update_index_in_dim(column_mass, after[1], target, 0)
                    return (row_high, row_mass, column_high, column_mass)

                def skipped(current):
                    return current

                return lax.cond(position < count, live, skipped, state), None

            start_state = (jnp.full((BLK,), floor_max, jnp.float32), jnp.zeros((BLK,), jnp.float32), columns[0], columns[1])
            final, unused = lax.scan(per_slot, start_state, jnp.arange(K, dtype=jnp.int32))
            return (final[2], final[3]), (final[0], final[1])

        start_columns = (jnp.full((NTB, BLK), floor_max, jnp.float32), jnp.zeros((NTB, BLK), jnp.float32))
        columns, rows = lax.scan(per_block, start_columns, (source_blocks, row_shift, pair_targets, pair_counts))
        new_rows = updated(row_potential, source_log_mass, source_squares, rows[0].reshape(-1), rows[1].reshape(-1))
        column_potential = updated(column_potential, target_log_mass, target_squares, columns[0].reshape(-1), columns[1].reshape(-1))
        row_potential = new_rows
    return row_potential, column_potential
```

```python
import functools
import jax
import jax.numpy as jnp
from jax import lax
from jax.experimental import pallas as pl
from jax.experimental.pallas import tpu as pltpu
from jax.sharding import PartitionSpec as P

ITERS = 2
epsilon = 0.5
absent = -1e30
log2e = 1.4426950408889634
headroom = 60.0
smallest = 1e-26
largest = 1e37
R = 256
NT = (((1,), (1,)), ((), ()))


def pieces(value):
    high = value.astype(jnp.bfloat16)
    rest = value - high.astype(jnp.float32)
    middle = rest.astype(jnp.bfloat16)
    low = (rest - middle.astype(jnp.float32)).astype(jnp.bfloat16)
    return high, middle, low


def lane_sums(block):
    ones = jnp.ones((8, block.shape[1]), jnp.bfloat16)
    total = None
    for part in pieces(block):
        product = lax.dot_general(ones, part, NT, preferred_element_type=jnp.float32)
        total = product if total is None else total + product
    return total[0:1]


def lane_first(block):
    lane = lax.broadcasted_iota(jnp.int32, (8, block.shape[1]), 1)
    pick = jnp.where(lane == 0, 1.0, 0.0).astype(jnp.bfloat16)
    total = None
    for part in pieces(block):
        product = lax.dot_general(pick, part, NT, preferred_element_type=jnp.float32)
        total = product if total is None else total + product
    return total[0:1]


def squares_row(points):
    wide = points.astype(jnp.float32)
    square = wide * wide
    high = square.astype(jnp.bfloat16)
    low = (square - high.astype(jnp.float32)).astype(jnp.bfloat16)
    ones = jnp.ones((8, points.shape[1]), jnp.bfloat16)
    total = lax.dot_general(ones, high, NT, preferred_element_type=jnp.float32)
    total = total + lax.dot_general(ones, low, NT, preferred_element_type=jnp.float32)
    return 0.5 * total[0:1]


def log_add(first, second):
    top = jnp.maximum(first, second)
    return top + jnp.log(jnp.exp(first - top) + jnp.exp(second - top))


def sweep_kernel(
    first_sweep,
    pair_targets, pair_counts, rank,
    points, *rest,
):
    if first_sweep:
        (targets, row_pot, col_pot,
         row_out, col_out, row_sq, col_sq,
         masks, listed, ybuf, features, row_acc, col_acc, slow_row, slow_col, full, sems) = rest
    else:
        (targets, row_pot, col_pot, row_sq, col_sq,
         row_out, col_out,
         masks, listed, ybuf, features, row_acc, col_acc, slow_row, slow_col, full, sems) = rest
    source_count, slot_width = pair_targets.shape
    target_count, block = col_pot.shape
    width = points.shape[1]
    base = rank[0] * target_count

    def clear(index, carry):
        masks[index] = 0
        return carry

    lax.fori_loop(0, target_count, clear, 0)

    def mark_source(source, carry):
        def mark(slot, inner):
            local = pair_targets[source, slot] - base

            @pl.when((local >= 0) & (local < target_count))
            def _():
                masks[local] = masks[local] | (1 << source)

            return inner

        return lax.fori_loop(0, pair_counts[source], mark, carry)

    lax.fori_loop(0, source_count, mark_source, 0)

    def collect(index, count):
        @pl.when(masks[index] != 0)
        def _():
            listed[count] = index

        return count + jnp.where(masks[index] != 0, 1, 0)

    active = lax.fori_loop(0, target_count, collect, 0)

    def fetch(position):
        slot = lax.rem(position, 2)
        start = pl.multiple_of(listed[position] * block, block)
        return pltpu.make_async_copy(
            targets.at[pl.ds(start, block), :], ybuf.at[slot], sems.at[slot]
        )

    @pl.when(active > 0)
    def _():
        fetch(0).start()

    if first_sweep:
        for source in range(source_count):
            row_sq[source : source + 1, :] = squares_row(points[source * block : (source + 1) * block, :])
    shifted = row_pot[...] - row_sq[...]
    parts = [part.astype(jnp.float32) for part in pieces(shifted)]
    pad = jnp.zeros((width - 3 * source_count, block), jnp.float32)
    features[...] = jnp.concatenate(parts + [pad], axis=0).T.astype(jnp.bfloat16)
    offset = (jnp.max(row_pot[...]) + jnp.max(col_pot[...])) / epsilon - headroom
    row_acc[...] = jnp.zeros_like(row_acc)
    col_acc[...] = jnp.zeros_like(col_acc)
    lane = lax.broadcasted_iota(jnp.int32, (1, width), 1)

    def pattern(source):
        chosen = (lax.rem(lane, source_count) == source) & (lane < 3 * source_count)
        return jnp.where(chosen, 1.0, 0.0).astype(jnp.bfloat16)

    def fast_tile(slot, target, source):
        ones_row = jnp.broadcast_to(pattern(source), (256, width))
        first_row = pl.multiple_of(source * block, block)
        for c in range(block // 256):
            cols = slice(c * 256, (c + 1) * 256)
            rhs = jnp.concatenate([ybuf[slot, cols, :], ones_row], axis=1)
            bias = full[0:1, cols]
            column = jnp.zeros((8, 256), jnp.float32)
            for r in range(block // R):
                rows = pl.ds(pl.multiple_of(first_row + r * R, R), R)
                lhs = jnp.concatenate([points[rows, :], features[r * R : (r + 1) * R, :]], axis=1)
                s = lax.dot_general(lhs, rhs, NT, preferred_element_type=jnp.float32)
                e = jnp.exp2(s * (log2e / epsilon) + bias)
                row_acc[rows, :] += e[:, :128] + e[:, 128:]
                column = column + jnp.sum(e.reshape(R // 8, 8, 256), axis=0)
            col_acc[target, :, cols] += column

    def slow_tile(slot, target, source):
        ones_row = jnp.broadcast_to(pattern(source), (256, width))
        first_row = pl.multiple_of(source * block, block)
        full[8:16, :] = jnp.full((8, block), absent, jnp.float32)

        def logits(r):
            rows = pl.ds(pl.multiple_of(first_row + r * 128, 128), 128)
            near = pl.ds(pl.multiple_of(r * 128, 128), 128)
            lhs = jnp.concatenate([points[rows, :], features[near, :]], axis=1)
            made = []
            for c in range(block // 256):
                rhs = jnp.concatenate([ybuf[slot, c * 256 : (c + 1) * 256, :], ones_row], axis=1)
                made.append(lax.dot_general(lhs, rhs, NT, preferred_element_type=jnp.float32))
            return rows, jnp.concatenate(made, axis=1) * (1.0 / epsilon) + full[0:1, :]

        def first_pass(r, carry):
            rows, t = logits(r)
            top = jnp.max(t, axis=1, keepdims=True)
            lse = top + jnp.log(jnp.sum(jnp.exp(t - top), axis=1, keepdims=True))
            slow_row[rows, :] = log_add(slow_row[rows, :], jnp.broadcast_to(lse, (128, width)))
            full[8:9, :] = jnp.maximum(full[8:9, :], jnp.max(t, axis=0, keepdims=True))
            return carry

        lax.fori_loop(0, block // 128, first_pass, 0)
        full[16:17, :] = jnp.zeros((1, block), jnp.float32)

        def second_pass(r, carry):
            rows, t = logits(r)
            full[16:17, :] += jnp.sum(jnp.exp(t - full[8:9, :]), axis=0, keepdims=True)
            return carry

        lax.fori_loop(0, block // 128, second_pass, 0)
        lse = full[8:9, :] + jnp.log(full[16:17, :])
        slow_col[pl.ds(target, 1), :] = log_add(slow_col[pl.ds(target, 1), :], lse)

    def over_pairs(tile, fast):
        def visit(position, carry):
            slot = lax.rem(position, 2)
            target = listed[position]
            fetch(position).wait()

            @pl.when(position + 1 < active)
            def _():
                fetch(position + 1).start()

            if first_sweep and fast:
                col_sq[pl.ds(target, 1), :] = squares_row(ybuf[slot])
            bias = (col_pot[pl.ds(target, 1), :] - col_sq[pl.ds(target, 1), :]) / epsilon
            full[0:1, :] = (bias - offset) * log2e if fast else bias
            mask = masks[target]

            def each(source, inner):
                @pl.when(((mask >> source) & 1) == 1)
                def _():
                    tile(slot, target, source)

                return inner

            return lax.fori_loop(0, source_count, each, carry)

        lax.fori_loop(0, active, visit, 0)

    over_pairs(fast_tile, True)

    col_sum = jnp.sum(col_acc[...], axis=1)
    row_sum = jnp.concatenate(
        [lane_sums(row_acc[s * block : (s + 1) * block, :]) for s in range(source_count)], axis=0
    )
    col_out[...] = jnp.where(col_sum > 0, jnp.log(col_sum) + offset, absent)
    row_out[...] = jnp.where(row_sum > 0, jnp.log(row_sum) + offset, absent)

    has_row = jnp.zeros(row_sum.shape, jnp.float32)
    row_id = lax.broadcasted_iota(jnp.int32, row_sum.shape, 0)
    col_id = lax.broadcasted_iota(jnp.int32, col_sum.shape, 0)
    union = lax.fori_loop(0, target_count, lambda i, m: m | masks[i], 0)
    row_live = ((union >> row_id) & 1) == 1

    def live_col(position, live):
        return jnp.where(col_id == listed[position], 1, live)

    col_live = lax.fori_loop(0, active, live_col, jnp.zeros(col_sum.shape, jnp.int32)) == 1
    row_bad = row_live & ~((row_sum > smallest) & (row_sum < largest))
    col_bad = col_live & ~((col_sum > smallest) & (col_sum < largest))
    bad = jnp.sum(row_bad.astype(jnp.float32)) + jnp.sum(col_bad.astype(jnp.float32))

    @pl.when(bad > 0)
    def _():
        slow_row[...] = jnp.full(slow_row.shape, absent, jnp.float32)
        slow_col[...] = jnp.full(slow_col.shape, absent, jnp.float32)
        fetch(0).start()
        over_pairs(slow_tile, False)
        col_out[...] = slow_col[...]
        for s in range(source_count):
            row_out[s : s + 1, :] = lane_first(slow_row[s * block : (s + 1) * block, :])


def sweep(first_sweep, pair_targets, pair_counts, rank, points, targets, row_pot, col_pot, *squares):
    source_count, block = row_pot.shape
    target_count = col_pot.shape[0]
    width = points.shape[1]
    vmem = pl.BlockSpec(memory_space=pltpu.VMEM)
    smem = pl.BlockSpec(memory_space=pltpu.SMEM)
    rows = jax.ShapeDtypeStruct(row_pot.shape, jnp.float32)
    cols = jax.ShapeDtypeStruct(col_pot.shape, jnp.float32)
    outs = (rows, cols, rows, cols) if first_sweep else (rows, cols)
    pairs = pair_targets.size // 4
    return pl.pallas_call(
        functools.partial(sweep_kernel, first_sweep),
        out_shape=outs,
        in_specs=[smem, smem, smem, vmem, pl.BlockSpec(memory_space=pl.ANY)] + [vmem] * (2 + len(squares)),
        out_specs=tuple(vmem for _ in outs),
        scratch_shapes=[
            pltpu.SMEM((target_count,), jnp.int32),
            pltpu.SMEM((target_count,), jnp.int32),
            pltpu.VMEM((2, block, width), jnp.bfloat16),
            pltpu.VMEM((block, width), jnp.bfloat16),
            pltpu.VMEM((source_count * block, width), jnp.float32),
            pltpu.VMEM((target_count, 8, block), jnp.float32),
            pltpu.VMEM((source_count * block, width), jnp.float32),
            pltpu.VMEM((target_count, block), jnp.float32),
            pltpu.VMEM((24, block), jnp.float32),
            pltpu.SemaphoreType.DMA((2,)),
        ],
        compiler_params=pltpu.CompilerParams(vmem_limit_bytes=40 * 1024 * 1024),
        cost_estimate=pl.CostEstimate(
            flops=2 * pairs * block * block * width,
            bytes_accessed=pairs * block * width * 2,
            transcendentals=pairs * block * block,
        ),
        name="sweep",
    )(pair_targets, pair_counts, rank, points, targets, row_pot, col_pot, *squares)


def exchange(value, axis, size):
    step = 1
    while step < size:
        other = lax.ppermute(value, axis, [(i, i ^ step) for i in range(size)])
        value = log_add(value, other)
        step *= 2
    return value


def local(
    source_points, target_points, source_potential, target_potential,
    source_log_mass, target_log_mass, pair_targets, pair_counts,
):
    source_count = pair_targets.shape[0]
    block = source_points.shape[0] // source_count
    src_size, tgt_size = lax.axis_size("src"), lax.axis_size("tgt")
    rank = lax.axis_index("tgt").astype(jnp.int32).reshape(1)
    row_pot = source_potential.reshape(source_count, block)
    col_pot = target_potential.reshape(-1, block)
    row_mass = source_log_mass.reshape(source_count, block)
    col_mass = target_log_mass.reshape(-1, block)
    squares = ()
    for iteration in range(ITERS):
        results = sweep(
            iteration == 0, pair_targets, pair_counts, rank,
            source_points, target_points, row_pot, col_pot, *squares,
        )
        if iteration == 0:
            squares = results[2:]
        rows = exchange(results[0], "tgt", tgt_size)
        cols = exchange(results[1], "src", src_size)
        row_pot = row_pot + (0.5 * epsilon) * (row_mass - rows)
        col_pot = col_pot + (0.5 * epsilon) * (col_mass - cols)
    return row_pot.reshape(-1), col_pot.reshape(-1)


def solution(mesh):
    placed = (
        P("src", None), P("tgt", None), P("src"), P("tgt"),
        P("src"), P("tgt"), P("src", None), P("src"),
    )
    return jax.shard_map(
        local, mesh=mesh, in_specs=placed, out_specs=(P("src"), P("tgt")), check_vma=False
    )
```

```python
import functools
import jax
import jax.numpy as jnp
from jax import lax
from jax.experimental import pallas as pl
from jax.experimental.pallas import tpu as pltpu
from jax.sharding import PartitionSpec as P

ITERS = 2
moved_cap = 16
epsilon = 0.5
absent = -1e30
log2e = 1.4426950408889634
headroom = 60.0
smallest = 1e-26
largest = 1e37
NT = (((1,), (1,)), ((), ()))


def pieces(value):
    high = value.astype(jnp.bfloat16)
    rest = value - high.astype(jnp.float32)
    middle = rest.astype(jnp.bfloat16)
    low = (rest - middle.astype(jnp.float32)).astype(jnp.bfloat16)
    return high, middle, low


def lane_sums(block):
    ones = jnp.ones((8, block.shape[1]), jnp.bfloat16)
    total = None
    for part in pieces(block):
        product = lax.dot_general(ones, part, NT, preferred_element_type=jnp.float32)
        total = product if total is None else total + product
    return total[0:1]


def lane_first(block):
    lane = lax.broadcasted_iota(jnp.int32, (8, block.shape[1]), 1)
    pick = jnp.where(lane == 0, 1.0, 0.0).astype(jnp.bfloat16)
    total = None
    for part in pieces(block):
        product = lax.dot_general(pick, part, NT, preferred_element_type=jnp.float32)
        total = product if total is None else total + product
    return total[0:1]


def log_add(first, second):
    top = jnp.maximum(first, second)
    return top + jnp.log(jnp.exp(first - top) + jnp.exp(second - top))


def bit_count(value):
    value = value - ((value >> 1) & 0x55555555)
    value = (value & 0x33333333) + ((value >> 2) & 0x33333333)
    value = (value + (value >> 4)) & 0x0F0F0F0F
    return (value * 0x01010101) >> 24


def plan_kernel(
    pair_targets, pair_counts, rank, targets,
    masks, listed, slots, meta, packed,
    both, loads, state, sems,
):
    source_count = pair_targets.shape[0]
    total = masks.shape[0]
    target_count = total // 2
    block = packed.shape[1]
    mine = lax.rem(rank[0], 2)
    base = (rank[0] - mine) * target_count

    def clear(index, carry):
        both[index] = 0
        masks[index] = 0
        return carry

    lax.fori_loop(0, total, clear, 0)
    loads[0] = 0
    loads[1] = 0

    def mark_source(source, carry):
        def mark(slot, inner):
            place = pair_targets[source, slot] - base

            @pl.when((place >= 0) & (place < total))
            def _():
                both[place] = both[place] | (1 << source)
                side = jnp.where(place >= target_count, 1, 0)
                loads[side] = loads[side] + 1

            return inner

        return lax.fori_loop(0, pair_counts[source], mark, carry)

    lax.fori_loop(0, source_count, mark_source, 0)
    heavy = jnp.where(loads[1] > loads[0], 1, 0)
    wanted = jnp.abs(loads[1] - loads[0]) // 2
    state[0] = 0
    state[1] = 0
    first = heavy * target_count
    giving = mine == heavy

    def keep_own(index, carry):
        masks[index] = both[mine * target_count + index]
        return carry

    lax.fori_loop(0, target_count, keep_own, 0)

    def offer(single):
        def consider(index, carry):
            mask = both[first + index]
            count = bit_count(mask)
            fits = (count == 1) if single else (count > 1)

            @pl.when(fits & (state[1] + count <= wanted) & (state[0] < packed.shape[0]))
            def _():
                place = state[0]
                slots[place] = index
                state[0] = place + 1
                state[1] = state[1] + count

                @pl.when(giving)
                def _():
                    masks[index] = 0
                    start = pl.multiple_of(index * block, block)
                    pltpu.make_async_copy(
                        targets.at[pl.ds(start, block), :], packed.at[place], sems.at[place]
                    ).start()

                @pl.when(jnp.logical_not(giving))
                def _():
                    masks[target_count + index] = mask

            return carry

        lax.fori_loop(0, target_count, consider, 0)

    offer(False)
    offer(True)

    def collect(index, carry):
        count, union = carry
        mask = masks[index]

        @pl.when(mask != 0)
        def _():
            listed[count] = index

        return count + jnp.where(mask != 0, 1, 0), union | mask

    own, union = lax.fori_loop(0, target_count, collect, (0, 0))
    foreign = jnp.where(giving, 0, state[0])

    def append(place, gathered):
        index = target_count + slots[place]
        listed[own + place] = index
        return gathered | masks[index]

    union = lax.fori_loop(0, foreign, append, union)
    meta[0] = own
    meta[1] = own + foreign
    meta[2] = union

    def finish(place, carry):
        pltpu.make_async_copy(
            targets.at[pl.ds(0, block), :], packed.at[place], sems.at[place]
        ).wait()
        return carry

    lax.fori_loop(0, jnp.where(giving, state[0], 0), finish, 0)


def plan(pair_targets, pair_counts, rank, targets, block):
    total = 2 * (targets.shape[0] // block)
    cap = min(moved_cap, total // 2)
    smem = pl.BlockSpec(memory_space=pltpu.SMEM)
    whole = jax.ShapeDtypeStruct((total,), jnp.int32)
    return pl.pallas_call(
        plan_kernel,
        out_shape=(
            whole, whole, jax.ShapeDtypeStruct((total,), jnp.int32), jax.ShapeDtypeStruct((8,), jnp.int32),
            jax.ShapeDtypeStruct((cap, block, targets.shape[1]), targets.dtype),
        ),
        in_specs=[smem, smem, smem, pl.BlockSpec(memory_space=pl.ANY)],
        out_specs=(smem, smem, smem, smem, pl.BlockSpec(memory_space=pltpu.VMEM)),
        scratch_shapes=[
            pltpu.SMEM((total,), jnp.int32),
            pltpu.SMEM((2,), jnp.int32),
            pltpu.SMEM((2,), jnp.int32),
            pltpu.SemaphoreType.DMA((cap,)),
        ],
        name="plan",
    )(pair_targets, pair_counts, rank, targets)


def sweep_kernel(
    masks, listed, meta, points, targets, foreign,
    row_pot, row_sq, col_pot, col_sq, far_pot, far_sq,
    row_out, col_out, far_out,
    ybuf, features, row_acc, col_acc, col_sum, faults, slow_row, full, sems,
):
    source_count, pieces_per, lanes = row_pot.shape
    target_count = col_pot.shape[0]
    block = pieces_per * lanes
    width = points.shape[1]
    own, active = meta[0], meta[1]

    def fetch_own(position):
        slot = lax.rem(position, 2)
        start = pl.multiple_of(listed[position] * block, block)
        return pltpu.make_async_copy(
            targets.at[pl.ds(start, block), :], ybuf.at[slot], sems.at[slot]
        )

    def fetch_foreign(position):
        slot = lax.rem(position, 2)
        return pltpu.make_async_copy(foreign.at[position - own], ybuf.at[slot], sems.at[slot])

    def start_fetch(position):
        @pl.when(position < own)
        def _():
            fetch_own(position).start()

        @pl.when((position >= own) & (position < active))
        def _():
            fetch_foreign(position).start()

    start_fetch(0)

    for h in range(pieces_per):
        shifted = row_pot[:, h, :] - row_sq[:, h, :]
        parts = [part.astype(jnp.float32) for part in pieces(shifted)]
        pad = jnp.zeros((width - 3 * source_count, lanes), jnp.float32)
        turned = jnp.concatenate(parts + [pad], axis=0).T
        features[h * lanes : (h + 1) * lanes, :] = turned.astype(jnp.bfloat16)
    tallest = jnp.maximum(jnp.max(col_pot[...]), jnp.max(far_pot[...]))
    offset = (jnp.max(row_pot[...]) + tallest) / epsilon - headroom
    row_acc[...] = jnp.zeros_like(row_acc)
    col_sum[...] = jnp.zeros_like(col_sum)
    faults[...] = jnp.zeros_like(faults)
    lane = lax.broadcasted_iota(jnp.int32, (1, width), 1)

    def pattern(source):
        chosen = (lax.rem(lane, source_count) == source) & (lane < 3 * source_count)
        return jnp.where(chosen, 1.0, 0.0).astype(jnp.bfloat16)

    def fast_tile(slot, target, source):
        ones_row = jnp.broadcast_to(pattern(source), (256, width))
        rows = pl.ds(pl.multiple_of(source * block, block), block)
        lhs = jnp.concatenate([points[rows, :], features[...]], axis=1)
        for c in range(block // 256):
            cols = slice(c * 256, (c + 1) * 256)
            rhs = jnp.concatenate([ybuf[slot, cols, :], ones_row], axis=1)
            s = lax.dot_general(lhs, rhs, NT, preferred_element_type=jnp.float32)
            e = jnp.exp2(s * (log2e / epsilon) + full[0:1, cols])
            row_acc[rows, :] += e[:, :128] + e[:, 128:]
            col_acc[:, cols] += jnp.sum(e.reshape(block // 8, 8, 256), axis=0)

    def fast_end(target):
        summed = jnp.sum(col_acc[...], axis=0, keepdims=True)
        safe = (summed > smallest) & (summed < largest)
        faults[0:1, :] = jnp.maximum(faults[0:1, :], jnp.where(safe, 0.0, 1.0))
        for h in range(pieces_per):
            col_sum[target, h : h + 1, :] = summed[:, h * lanes : (h + 1) * lanes]

    def slow_tile(slot, target, source):
        ones_row = jnp.broadcast_to(pattern(source), (256, width))
        first_row = pl.multiple_of(source * block, block)
        full[8:16, :] = jnp.full((8, block), absent, jnp.float32)

        def logits(r):
            rows = pl.ds(pl.multiple_of(first_row + r * 128, 128), 128)
            near = pl.ds(pl.multiple_of(r * 128, 128), 128)
            lhs = jnp.concatenate([points[rows, :], features[near, :]], axis=1)
            made = []
            for c in range(block // 256):
                rhs = jnp.concatenate([ybuf[slot, c * 256 : (c + 1) * 256, :], ones_row], axis=1)
                made.append(lax.dot_general(lhs, rhs, NT, preferred_element_type=jnp.float32))
            return rows, jnp.concatenate(made, axis=1) * (1.0 / epsilon) + full[0:1, :]

        def first_pass(r, carry):
            rows, t = logits(r)
            top = jnp.max(t, axis=1, keepdims=True)
            lse = top + jnp.log(jnp.sum(jnp.exp(t - top), axis=1, keepdims=True))
            slow_row[rows, :] = log_add(slow_row[rows, :], jnp.broadcast_to(lse, (128, width)))
            full[8:9, :] = jnp.maximum(full[8:9, :], jnp.max(t, axis=0, keepdims=True))
            return carry

        lax.fori_loop(0, block // 128, first_pass, 0)
        full[16:17, :] = jnp.zeros((1, block), jnp.float32)

        def second_pass(r, carry):
            rows, t = logits(r)
            full[16:17, :] += jnp.sum(jnp.exp(t - full[8:9, :]), axis=0, keepdims=True)
            return carry

        lax.fori_loop(0, block // 128, second_pass, 0)
        lse = full[8:9, :] + jnp.log(full[16:17, :])
        col_acc[0:1, :] = log_add(col_acc[0:1, :], lse)

    def slow_end(target):
        for h in range(pieces_per):
            col_sum[target, h : h + 1, :] = col_acc[0:1, h * lanes : (h + 1) * lanes]

    def over_pairs(tile, end, fast):
        def visit(position, carry):
            slot = lax.rem(position, 2)
            target = listed[position]
            fetch_wait(slot)
            start_fetch(position + 1)
            near = jnp.minimum(target, target_count - 1)
            far = jnp.maximum(target - target_count, 0)
            bias = jnp.where(
                target < target_count,
                col_pot[near] - col_sq[near],
                far_pot[far] - far_sq[far],
            ) / epsilon
            bias = (bias - offset) * log2e if fast else bias
            for h in range(pieces_per):
                full[0:1, h * lanes : (h + 1) * lanes] = bias[h : h + 1, :]
            col_acc[...] = jnp.full(col_acc.shape, 0.0 if fast else absent, jnp.float32)
            mask = masks[target]

            def each(source, inner):
                @pl.when(((mask >> source) & 1) == 1)
                def _():
                    tile(slot, target, source)

                return inner

            lax.fori_loop(0, source_count, each, 0)
            end(target)
            return carry

        lax.fori_loop(0, active, visit, 0)

    def fetch_wait(slot):
        pltpu.make_async_copy(targets.at[pl.ds(0, block), :], ybuf.at[slot], sems.at[slot]).wait()

    over_pairs(fast_tile, fast_end, True)

    def put_rows(source, row):
        for h in range(pieces_per):
            row_out[source, h : h + 1, :] = row[:, h * lanes : (h + 1) * lanes]

    for source in range(source_count):
        summed = lane_sums(row_acc[source * block : (source + 1) * block, :])
        wanted = ((meta[2] >> source) & 1) == 1
        safe = ((summed > smallest) & (summed < largest)) | jnp.logical_not(wanted)
        faults[0:1, :] = jnp.maximum(faults[0:1, :], jnp.where(safe, 0.0, 1.0))
        put_rows(source, jnp.where(summed > 0, jnp.log(summed) + offset, absent))
    sums = col_sum[...]
    made = jnp.where(sums > 0, jnp.log(sums) + offset, absent)
    col_out[...] = made[:target_count]
    far_out[...] = made[target_count:]

    @pl.when(jnp.max(faults[0:1, :]) > 0)
    def _():
        slow_row[...] = jnp.full(slow_row.shape, absent, jnp.float32)
        col_sum[...] = jnp.full(col_sum.shape, absent, jnp.float32)
        start_fetch(0)
        over_pairs(slow_tile, slow_end, False)
        col_out[...] = col_sum[:target_count]
        far_out[...] = col_sum[target_count:]
        for source in range(source_count):
            put_rows(source, lane_first(slow_row[source * block : (source + 1) * block, :]))


def sweep(masks, listed, meta, points, targets, foreign, *cells):
    row_pot, col_pot = cells[0], cells[2]
    source_count, pieces_per, lanes = row_pot.shape
    target_count = col_pot.shape[0]
    block = pieces_per * lanes
    width = points.shape[1]
    vmem = pl.BlockSpec(memory_space=pltpu.VMEM)
    smem = pl.BlockSpec(memory_space=pltpu.SMEM)
    anywhere = pl.BlockSpec(memory_space=pl.ANY)
    rows = jax.ShapeDtypeStruct(row_pot.shape, jnp.float32)
    cols = jax.ShapeDtypeStruct(col_pot.shape, jnp.float32)
    pairs = 3 * source_count
    return pl.pallas_call(
        sweep_kernel,
        out_shape=(rows, cols, cols),
        in_specs=[smem, smem, smem, vmem, anywhere, anywhere] + [vmem] * len(cells),
        out_specs=(vmem, vmem, vmem),
        scratch_shapes=[
            pltpu.VMEM((2, block, width), jnp.bfloat16),
            pltpu.VMEM((block, width), jnp.bfloat16),
            pltpu.VMEM((source_count * block, width), jnp.float32),
            pltpu.VMEM((8, block), jnp.float32),
            pltpu.VMEM((2 * target_count, pieces_per, lanes), jnp.float32),
            pltpu.VMEM((8, block), jnp.float32),
            pltpu.VMEM((source_count * block, width), jnp.float32),
            pltpu.VMEM((24, block), jnp.float32),
            pltpu.SemaphoreType.DMA((2,)),
        ],
        compiler_params=pltpu.CompilerParams(vmem_limit_bytes=40 * 1024 * 1024),
        cost_estimate=pl.CostEstimate(
            flops=2 * pairs * block * block * width,
            bytes_accessed=pairs * block * width * 2,
            transcendentals=pairs * block * block,
        ),
        name="sweep",
    )(masks, listed, meta, points, targets, foreign, *cells)


def swapped(value, axis, size, step):
    return lax.ppermute(value, axis, [(i, i ^ step) for i in range(size)])


def exchange(value, axis, size):
    if size == 1:
        return value
    half = value.shape[0] // 2
    low = lax.rem(lax.axis_index(axis), 2)
    kept = lax.dynamic_slice_in_dim(value, low * half, half, 0)
    sent = lax.dynamic_slice_in_dim(value, (1 - low) * half, half, 0)
    kept = log_add(kept, swapped(sent, axis, size, 1))
    step = 2
    while step < size:
        kept = log_add(kept, swapped(kept, axis, size, step))
        step *= 2
    other = swapped(kept, axis, size, 1)
    return jnp.where(
        low == 0, jnp.concatenate([kept, other], axis=0), jnp.concatenate([other, kept], axis=0)
    )


def doubled(value, axis, size):
    step = 1
    while step < size:
        value = log_add(value, swapped(value, axis, size, step))
        step *= 2
    return value


def half_squares(points):
    widened = points.astype(jnp.float32)
    return 0.5 * jnp.sum(widened * widened, axis=1)


def local(
    source_points, target_points, source_potential, target_potential,
    source_log_mass, target_log_mass, pair_targets, pair_counts,
):
    source_count = pair_targets.shape[0]
    block = source_points.shape[0] // source_count
    src_size, tgt_size = lax.axis_size("src"), lax.axis_size("tgt")
    rank = lax.axis_index("tgt").astype(jnp.int32).reshape(1)

    def by_block(value):
        return value.reshape(-1, block // 128, 128)

    masks, listed, _, meta, packed = plan(pair_targets, pair_counts, rank, target_points, block)
    foreign = swapped(packed, "tgt", tgt_size, 1)
    row_pot, col_pot = by_block(source_potential), by_block(target_potential)
    row_mass, col_mass = by_block(source_log_mass), by_block(target_log_mass)
    row_sq, col_sq = by_block(half_squares(source_points)), by_block(half_squares(target_points))
    far_sq = swapped(col_sq, "tgt", tgt_size, 1)
    for _ in range(ITERS):
        far_pot = swapped(col_pot, "tgt", tgt_size, 1)
        rows, cols, far = sweep(
            masks, listed, meta, source_points, target_points, foreign,
            row_pot, row_sq, col_pot, col_sq, far_pot, far_sq,
        )
        cols = log_add(cols, swapped(far, "tgt", tgt_size, 1))
        rows = doubled(rows, "tgt", tgt_size)
        cols = exchange(cols, "src", src_size)
        row_pot = row_pot + (0.5 * epsilon) * (row_mass - rows)
        col_pot = col_pot + (0.5 * epsilon) * (col_mass - cols)
    return row_pot.reshape(-1), col_pot.reshape(-1)


def solution(mesh):
    placed = (
        P("src", None), P("tgt", None), P("src"), P("tgt"),
        P("src"), P("tgt"), P("src", None), P("src"),
    )
    return jax.shard_map(
        local, mesh=mesh, in_specs=placed, out_specs=(P("src"), P("tgt")), check_vma=False
    )
```

```python
import functools
import jax
import jax.numpy as jnp
from jax import lax
from jax.experimental import pallas as pl
from jax.experimental.pallas import tpu as pltpu
from jax.sharding import PartitionSpec as P

ITERS = 2
moved_cap = 8
epsilon = 0.5
absent = -1e30
log2e = 1.4426950408889634
headroom = 60.0
smallest = 1e-26
largest = 1e37
NT = (((1,), (1,)), ((), ()))


def pieces(value):
    high = value.astype(jnp.bfloat16)
    rest = value - high.astype(jnp.float32)
    middle = rest.astype(jnp.bfloat16)
    low = (rest - middle.astype(jnp.float32)).astype(jnp.bfloat16)
    return high, middle, low


def two_pieces(value):
    high = value.astype(jnp.bfloat16)
    low = (value - high.astype(jnp.float32)).astype(jnp.bfloat16)
    return jnp.concatenate([high, low], axis=1)


def lane_sums(block):
    ones = jnp.ones((8, 2 * block.shape[1]), jnp.bfloat16)
    return lax.dot_general(ones, two_pieces(block), NT, preferred_element_type=jnp.float32)[0:1]


def lane_first(block):
    lane = lax.broadcasted_iota(jnp.int32, (8, block.shape[1]), 1)
    pick = jnp.where(lane == 0, 1.0, 0.0).astype(jnp.bfloat16)
    total = None
    for part in pieces(block):
        product = lax.dot_general(pick, part, NT, preferred_element_type=jnp.float32)
        total = product if total is None else total + product
    return total[0:1]


def log_add(first, second):
    top = jnp.maximum(first, second)
    return top + jnp.log(jnp.exp(first - top) + jnp.exp(second - top))


def bit_count(value):
    value = value - ((value >> 1) & 0x55555555)
    value = (value & 0x33333333) + ((value >> 2) & 0x33333333)
    value = (value + (value >> 4)) & 0x0F0F0F0F
    return (value * 0x01010101) >> 24


def plan_kernel(
    pair_targets, pair_counts, rank, targets,
    masks, listed, meta, packed,
    both, slots, state, sems,
):
    source_count, slot_width = pair_targets.shape
    total = both.shape[0] - 1
    target_count = total // 2
    block = packed.shape[1]
    mine = lax.rem(rank[0], 2)
    base = (rank[0] - mine) * target_count
    for index in range(total + 1):
        both[index] = 0
    low_load = jnp.int32(0)
    high_load = jnp.int32(0)
    for source in range(source_count):
        count = pair_counts[source]
        for slot in range(slot_width):
            place = pair_targets[source, slot] - base
            named = (slot < count) & (place >= 0) & (place < total)
            index = jnp.where(named, place, total)
            both[index] = both[index] | (1 << source)
            low_load = low_load + jnp.where(named & (place < target_count), 1, 0)
            high_load = high_load + jnp.where(named & (place >= target_count), 1, 0)
    heavy = jnp.where(high_load > low_load, 1, 0)
    wanted = jnp.abs(high_load - low_load) // 2
    state[0] = 0
    state[1] = 0
    first = heavy * target_count
    giving = mine == heavy

    def offer(single):
        def consider(index, carry):
            mask = both[first + index]
            rest = mask & (mask - 1)
            apt = ((mask != 0) & (rest == 0)) if single else (rest != 0)

            @pl.when(apt & (state[0] < packed.shape[0]))
            def _():
                count = 1 if single else bit_count(mask)

                @pl.when(state[1] + count <= wanted)
                def _():
                    place = state[0]
                    state[0] = place + 1
                    state[1] = state[1] + count

                    @pl.when(giving)
                    def _():
                        both[first + index] = 0
                        start = pl.multiple_of(index * block, block)
                        pltpu.make_async_copy(
                            targets.at[pl.ds(start, block), :], packed.at[place], sems.at[place]
                        ).start()

                    @pl.when(jnp.logical_not(giving))
                    def _():
                        slots[place] = target_count + index
                        masks[target_count + index] = mask

            return carry

        lax.fori_loop(0, target_count, consider, 0)

    offer(False)
    offer(True)
    count = jnp.int32(0)
    union = jnp.int32(0)
    for index in range(target_count):
        mask = both[mine * target_count + index]
        masks[index] = mask
        listed[count] = index
        count = count + jnp.where(mask != 0, 1, 0)
        union = union | mask
    own = count
    foreign = jnp.where(giving, 0, state[0])

    def append(place, gathered):
        index = slots[place]
        listed[own + place] = index
        return gathered | masks[index]

    union = lax.fori_loop(0, foreign, append, union)
    meta[0] = own
    meta[1] = own + foreign
    meta[2] = union

    def finish(place, carry):
        pltpu.make_async_copy(
            targets.at[pl.ds(0, block), :], packed.at[place], sems.at[place]
        ).wait()
        return carry

    lax.fori_loop(0, jnp.where(giving, state[0], 0), finish, 0)


def plan(pair_targets, pair_counts, rank, targets, block):
    total = 2 * (targets.shape[0] // block)
    cap = min(moved_cap, total // 2)
    smem = pl.BlockSpec(memory_space=pltpu.SMEM)
    table = jax.ShapeDtypeStruct((total + 1,), jnp.int32)
    return pl.pallas_call(
        plan_kernel,
        out_shape=(
            table, table, jax.ShapeDtypeStruct((8,), jnp.int32),
            jax.ShapeDtypeStruct((cap, block, targets.shape[1]), targets.dtype),
        ),
        in_specs=[smem, smem, smem, pl.BlockSpec(memory_space=pl.ANY)],
        out_specs=(smem, smem, smem, pl.BlockSpec(memory_space=pltpu.VMEM)),
        scratch_shapes=[
            pltpu.SMEM((total + 1,), jnp.int32),
            pltpu.SMEM((cap,), jnp.int32),
            pltpu.SMEM((2,), jnp.int32),
            pltpu.SemaphoreType.DMA((cap,)),
        ],
        name="plan",
    )(pair_targets, pair_counts, rank, targets)


def squares_kernel(points, out):
    count, pieces_per, lanes = out.shape
    block = pieces_per * lanes
    ones = jnp.ones((8, 2 * points.shape[1]), jnp.bfloat16)
    for index in range(count):
        wide = points[index * block : (index + 1) * block, :].astype(jnp.float32)
        summed = lax.dot_general(
            ones, two_pieces(wide * wide), NT, preferred_element_type=jnp.float32
        )
        for h in range(pieces_per):
            out[index, h : h + 1, :] = 0.5 * summed[0:1, h * lanes : (h + 1) * lanes]


def half_squares(points, block):
    count = points.shape[0] // block
    group = 8 if count % 8 == 0 else 1
    return pl.pallas_call(
        squares_kernel,
        grid=(count // group,),
        out_shape=jax.ShapeDtypeStruct((count, block // 128, 128), jnp.float32),
        in_specs=[pl.BlockSpec((group * block, points.shape[1]), lambda i: (i, 0))],
        out_specs=pl.BlockSpec((group, block // 128, 128), lambda i: (i, 0, 0)),
        cost_estimate=pl.CostEstimate(
            flops=2 * points.size, bytes_accessed=2 * points.size, transcendentals=0
        ),
        name="squares",
    )(points)


def sweep_kernel(
    masks, listed, meta, stored, targets, foreign,
    row_pot, row_sq, col_pot, col_sq, far_pot, far_sq,
    row_out, col_out, far_out,
    points, ybuf, features, row_acc, col_acc, col_sum, faults, slow_row, full, sems, point_sem,
):
    source_count, pieces_per, lanes = row_pot.shape
    target_count = col_pot.shape[0]
    block = pieces_per * lanes
    width = points.shape[1]
    own, active = meta[0], meta[1]

    def fetch_own(position):
        slot = lax.rem(position, 2)
        start = pl.multiple_of(listed[position] * block, block)
        return pltpu.make_async_copy(
            targets.at[pl.ds(start, block), :], ybuf.at[slot], sems.at[slot]
        )

    def fetch_foreign(position):
        slot = lax.rem(position, 2)
        return pltpu.make_async_copy(foreign.at[position - own], ybuf.at[slot], sems.at[slot])

    def start_fetch(position):
        @pl.when(position < own)
        def _():
            fetch_own(position).start()

        @pl.when((position >= own) & (position < active))
        def _():
            fetch_foreign(position).start()

    bring = pltpu.make_async_copy(stored, points, point_sem)
    bring.start()
    start_fetch(0)

    for h in range(pieces_per):
        shifted = row_pot[:, h, :] - row_sq[:, h, :]
        parts = [part.astype(jnp.float32) for part in pieces(shifted)]
        pad = jnp.zeros((width - 3 * source_count, lanes), jnp.float32)
        turned = jnp.concatenate(parts + [pad], axis=0).T
        features[h * lanes : (h + 1) * lanes, :] = turned.astype(jnp.bfloat16)
    tallest = jnp.maximum(jnp.max(col_pot[...]), jnp.max(far_pot[...]))
    offset = (jnp.max(row_pot[...]) + tallest) / epsilon - headroom
    row_acc[...] = jnp.zeros_like(row_acc)
    col_sum[...] = jnp.zeros_like(col_sum)
    faults[...] = jnp.zeros_like(faults)
    lane = lax.broadcasted_iota(jnp.int32, (1, width), 1)

    def pattern(source):
        chosen = (lax.rem(lane, source_count) == source) & (lane < 3 * source_count)
        return jnp.where(chosen, 1.0, 0.0).astype(jnp.bfloat16)

    def fast_tile(slot, target, source):
        ones_row = jnp.broadcast_to(pattern(source), (256, width))
        rows = pl.ds(pl.multiple_of(source * block, block), block)
        lhs = jnp.concatenate([points[rows, :], features[...]], axis=1)
        for c in range(block // 256):
            cols = slice(c * 256, (c + 1) * 256)
            rhs = jnp.concatenate([ybuf[slot, cols, :], ones_row], axis=1)
            s = lax.dot_general(lhs, rhs, NT, preferred_element_type=jnp.float32)
            e = jnp.exp2(s * (log2e / epsilon) + full[0:1, cols])
            row_acc[rows, :] += e[:, :128] + e[:, 128:]
            col_acc[:, cols] += jnp.sum(e.reshape(block // 8, 8, 256), axis=0)

    def fast_end(target):
        summed = jnp.sum(col_acc[...], axis=0, keepdims=True)
        safe = (summed > smallest) & (summed < largest)
        faults[0:1, :] = jnp.maximum(faults[0:1, :], jnp.where(safe, 0.0, 1.0))
        for h in range(pieces_per):
            col_sum[target, h : h + 1, :] = summed[:, h * lanes : (h + 1) * lanes]

    def slow_tile(slot, target, source):
        ones_row = jnp.broadcast_to(pattern(source), (256, width))
        first_row = pl.multiple_of(source * block, block)
        full[8:16, :] = jnp.full((8, block), absent, jnp.float32)

        def logits(r):
            rows = pl.ds(pl.multiple_of(first_row + r * 128, 128), 128)
            near = pl.ds(pl.multiple_of(r * 128, 128), 128)
            lhs = jnp.concatenate([points[rows, :], features[near, :]], axis=1)
            made = []
            for c in range(block // 256):
                rhs = jnp.concatenate([ybuf[slot, c * 256 : (c + 1) * 256, :], ones_row], axis=1)
                made.append(lax.dot_general(lhs, rhs, NT, preferred_element_type=jnp.float32))
            return rows, jnp.concatenate(made, axis=1) * (1.0 / epsilon) + full[0:1, :]

        def first_pass(r, carry):
            rows, t = logits(r)
            top = jnp.max(t, axis=1, keepdims=True)
            lse = top + jnp.log(jnp.sum(jnp.exp(t - top), axis=1, keepdims=True))
            slow_row[rows, :] = log_add(slow_row[rows, :], jnp.broadcast_to(lse, (128, width)))
            full[8:9, :] = jnp.maximum(full[8:9, :], jnp.max(t, axis=0, keepdims=True))
            return carry

        lax.fori_loop(0, block // 128, first_pass, 0)
        full[16:17, :] = jnp.zeros((1, block), jnp.float32)

        def second_pass(r, carry):
            rows, t = logits(r)
            full[16:17, :] += jnp.sum(jnp.exp(t - full[8:9, :]), axis=0, keepdims=True)
            return carry

        lax.fori_loop(0, block // 128, second_pass, 0)
        lse = full[8:9, :] + jnp.log(full[16:17, :])
        col_acc[0:1, :] = log_add(col_acc[0:1, :], lse)

    def slow_end(target):
        for h in range(pieces_per):
            col_sum[target, h : h + 1, :] = col_acc[0:1, h * lanes : (h + 1) * lanes]

    def over_pairs(tile, end, fast):
        def visit(position, carry):
            slot = lax.rem(position, 2)
            target = listed[position]
            fetch_wait(slot)
            start_fetch(position + 1)
            near = jnp.minimum(target, target_count - 1)
            far = jnp.maximum(target - target_count, 0)
            bias = jnp.where(
                target < target_count,
                col_pot[near] - col_sq[near],
                far_pot[far] - far_sq[far],
            ) / epsilon
            bias = (bias - offset) * log2e if fast else bias
            for h in range(pieces_per):
                full[0:1, h * lanes : (h + 1) * lanes] = bias[h : h + 1, :]
            col_acc[...] = jnp.full(col_acc.shape, 0.0 if fast else absent, jnp.float32)
            mask = masks[target]

            def each(source, inner):
                @pl.when(((mask >> source) & 1) == 1)
                def _():
                    tile(slot, target, source)

                return inner

            lax.fori_loop(0, source_count, each, 0)
            end(target)
            return carry

        lax.fori_loop(0, active, visit, 0)

    def fetch_wait(slot):
        pltpu.make_async_copy(targets.at[pl.ds(0, block), :], ybuf.at[slot], sems.at[slot]).wait()

    bring.wait()
    over_pairs(fast_tile, fast_end, True)

    def put_rows(source, row):
        for h in range(pieces_per):
            row_out[source, h : h + 1, :] = row[:, h * lanes : (h + 1) * lanes]

    for source in range(source_count):
        summed = lane_sums(row_acc[source * block : (source + 1) * block, :])
        wanted = ((meta[2] >> source) & 1) == 1
        safe = ((summed > smallest) & (summed < largest)) | jnp.logical_not(wanted)
        faults[0:1, :] = jnp.maximum(faults[0:1, :], jnp.where(safe, 0.0, 1.0))
        put_rows(source, jnp.where(summed > 0, jnp.log(summed) + offset, absent))
    sums = col_sum[...]
    made = jnp.where(sums > 0, jnp.log(sums) + offset, absent)
    col_out[...] = made[:target_count]
    far_out[...] = made[target_count:]

    @pl.when(jnp.max(faults[0:1, :]) > 0)
    def _():
        slow_row[...] = jnp.full(slow_row.shape, absent, jnp.float32)
        col_sum[...] = jnp.full(col_sum.shape, absent, jnp.float32)
        start_fetch(0)
        over_pairs(slow_tile, slow_end, False)
        col_out[...] = col_sum[:target_count]
        far_out[...] = col_sum[target_count:]
        for source in range(source_count):
            put_rows(source, lane_first(slow_row[source * block : (source + 1) * block, :]))


def sweep(masks, listed, meta, points, targets, foreign, *cells):
    row_pot, col_pot = cells[0], cells[2]
    source_count, pieces_per, lanes = row_pot.shape
    target_count = col_pot.shape[0]
    block = pieces_per * lanes
    width = points.shape[1]
    vmem = pl.BlockSpec(memory_space=pltpu.VMEM)
    smem = pl.BlockSpec(memory_space=pltpu.SMEM)
    anywhere = pl.BlockSpec(memory_space=pl.ANY)
    rows = jax.ShapeDtypeStruct(row_pot.shape, jnp.float32)
    cols = jax.ShapeDtypeStruct(col_pot.shape, jnp.float32)
    pairs = 3 * source_count
    return pl.pallas_call(
        sweep_kernel,
        out_shape=(rows, cols, cols),
        in_specs=[smem, smem, smem, anywhere, anywhere, anywhere] + [vmem] * len(cells),
        out_specs=(vmem, vmem, vmem),
        scratch_shapes=[
            pltpu.VMEM(points.shape, points.dtype),
            pltpu.VMEM((2, block, width), jnp.bfloat16),
            pltpu.VMEM((block, width), jnp.bfloat16),
            pltpu.VMEM((source_count * block, width), jnp.float32),
            pltpu.VMEM((8, block), jnp.float32),
            pltpu.VMEM((2 * target_count, pieces_per, lanes), jnp.float32),
            pltpu.VMEM((8, block), jnp.float32),
            pltpu.VMEM((source_count * block, width), jnp.float32),
            pltpu.VMEM((24, block), jnp.float32),
            pltpu.SemaphoreType.DMA((2,)),
            pltpu.SemaphoreType.DMA,
        ],
        compiler_params=pltpu.CompilerParams(vmem_limit_bytes=40 * 1024 * 1024),
        cost_estimate=pl.CostEstimate(
            flops=2 * pairs * block * block * width,
            bytes_accessed=pairs * block * width * 2,
            transcendentals=pairs * block * block,
        ),
        name="sweep",
    )(masks, listed, meta, points, targets, foreign, *cells)


def swapped(value, axis, size, step):
    return lax.ppermute(value, axis, [(i, i ^ step) for i in range(size)])


def exchange(value, axis, size):
    steps = []
    while 2 ** len(steps) < size:
        steps.append(2 ** len(steps))
    if not steps:
        return value
    me = lax.axis_index(axis)
    share = value.shape[0] // 4
    parts = [value[: 2 * share], value[2 * share :]]
    orders = [steps, steps[1:] + steps[:1]]
    lows = [lax.rem(me // order[0], 2) for order in orders]
    for turn in range(len(steps)):
        for at in range(2):
            step = orders[at][turn]
            if turn == 0:
                kept = lax.dynamic_slice_in_dim(parts[at], lows[at] * share, share, 0)
                sent = lax.dynamic_slice_in_dim(parts[at], (1 - lows[at]) * share, share, 0)
            else:
                kept = sent = parts[at]
            parts[at] = log_add(kept, swapped(sent, axis, size, step))
    joined = []
    for at in range(2):
        other = swapped(parts[at], axis, size, orders[at][0])
        first = lows[at] == 0
        joined += [jnp.where(first, parts[at], other), jnp.where(first, other, parts[at])]
    return jnp.concatenate(joined, axis=0)


def doubled(value, axis, size):
    step = 1
    while step < size:
        value = log_add(value, swapped(value, axis, size, step))
        step *= 2
    return value


def local(
    source_points, target_points, source_potential, target_potential,
    source_log_mass, target_log_mass, pair_targets, pair_counts,
):
    source_count = pair_targets.shape[0]
    block = source_points.shape[0] // source_count
    src_size, tgt_size = lax.axis_size("src"), lax.axis_size("tgt")
    rank = lax.axis_index("tgt").astype(jnp.int32).reshape(1)

    def by_block(value):
        return value.reshape(-1, block // 128, 128)

    masks, listed, meta, packed = plan(pair_targets, pair_counts, rank, target_points, block)
    foreign = swapped(packed, "tgt", tgt_size, 1)
    row_pot, col_pot = by_block(source_potential), by_block(target_potential)
    row_mass, col_mass = by_block(source_log_mass), by_block(target_log_mass)
    row_sq, col_sq = half_squares(source_points, block), half_squares(target_points, block)
    far_sq = swapped(col_sq, "tgt", tgt_size, 1)
    for _ in range(ITERS):
        far_pot = swapped(col_pot, "tgt", tgt_size, 1)
        rows, cols, far = sweep(
            masks, listed, meta, source_points, target_points, foreign,
            row_pot, row_sq, col_pot, col_sq, far_pot, far_sq,
        )
        cols = log_add(cols, swapped(far, "tgt", tgt_size, 1))
        rows = doubled(rows, "tgt", tgt_size)
        cols = exchange(cols, "src", src_size)
        row_pot = row_pot + (0.5 * epsilon) * (row_mass - rows)
        col_pot = col_pot + (0.5 * epsilon) * (col_mass - cols)
    return row_pot.reshape(-1), col_pot.reshape(-1)


def solution(mesh):
    placed = (
        P("src", None), P("tgt", None), P("src"), P("tgt"),
        P("src"), P("tgt"), P("src", None), P("src"),
    )
    return jax.shard_map(
        local, mesh=mesh, in_specs=placed, out_specs=(P("src"), P("tgt")), check_vma=False
    )
```

```python
import functools
import jax
import jax.numpy as jnp
from jax import lax
from jax.experimental import pallas as pl
from jax.experimental.pallas import tpu as pltpu
from jax.sharding import PartitionSpec as P

ITERS = 2
moved_cap = 8
epsilon = 0.5
absent = -1e30
log2e = 1.4426950408889634
headroom = 60.0
smallest = 1e-26
largest = 1e37
NT = (((1,), (1,)), ((), ()))


def pieces(value):
    high = value.astype(jnp.bfloat16)
    rest = value - high.astype(jnp.float32)
    middle = rest.astype(jnp.bfloat16)
    low = (rest - middle.astype(jnp.float32)).astype(jnp.bfloat16)
    return high, middle, low


def two_pieces(value):
    high = value.astype(jnp.bfloat16)
    low = (value - high.astype(jnp.float32)).astype(jnp.bfloat16)
    return jnp.concatenate([high, low], axis=1)


def lane_sums(block):
    ones = jnp.ones((8, 2 * block.shape[1]), jnp.bfloat16)
    return lax.dot_general(ones, two_pieces(block), NT, preferred_element_type=jnp.float32)[0:1]


def lane_first(block):
    lane = lax.broadcasted_iota(jnp.int32, (8, block.shape[1]), 1)
    pick = jnp.where(lane == 0, 1.0, 0.0).astype(jnp.bfloat16)
    total = None
    for part in pieces(block):
        product = lax.dot_general(pick, part, NT, preferred_element_type=jnp.float32)
        total = product if total is None else total + product
    return total[0:1]


def log_add(first, second):
    top = jnp.maximum(first, second)
    return top + jnp.log(jnp.exp(first - top) + jnp.exp(second - top))


def bit_count(value):
    value = value - ((value >> 1) & 0x55555555)
    value = (value & 0x33333333) + ((value >> 2) & 0x33333333)
    value = (value + (value >> 4)) & 0x0F0F0F0F
    return (value * 0x01010101) >> 24


def plan_kernel(
    pair_targets, pair_counts, rank, targets,
    masks, listed, meta, named_blocks, packed,
    both, slots, state, sems,
):
    source_count, slot_width = pair_targets.shape
    total = both.shape[0] - 1
    target_count = total // 2
    block = packed.shape[1]
    mine = lax.rem(rank[0], 2)
    base = (rank[0] - mine) * target_count
    for index in range(total + 1):
        both[index] = 0
    low_load = jnp.int32(0)
    high_load = jnp.int32(0)
    for source in range(source_count):
        count = pair_counts[source]
        for slot in range(slot_width):
            place = pair_targets[source, slot] - base
            here = (slot < count) & (place >= 0) & (place < total)
            index = jnp.where(here, place, total)
            both[index] = both[index] | (1 << source)
            low_load = low_load + jnp.where(here & (place < target_count), 1, 0)
            high_load = high_load + jnp.where(here & (place >= target_count), 1, 0)
    named = jnp.int32(0)
    for index in range(target_count):
        named_blocks[named] = index
        named = named + jnp.where(both[mine * target_count + index] != 0, 1, 0)
    meta[3] = named
    heavy = jnp.where(high_load > low_load, 1, 0)
    wanted = jnp.abs(high_load - low_load) // 2
    state[0] = 0
    state[1] = 0
    first = heavy * target_count
    giving = mine == heavy

    def offer(single):
        def consider(index, carry):
            mask = both[first + index]
            rest = mask & (mask - 1)
            apt = ((mask != 0) & (rest == 0)) if single else (rest != 0)

            @pl.when(apt & (state[0] < packed.shape[0]))
            def _():
                count = 1 if single else bit_count(mask)

                @pl.when(state[1] + count <= wanted)
                def _():
                    place = state[0]
                    state[0] = place + 1
                    state[1] = state[1] + count

                    @pl.when(giving)
                    def _():
                        both[first + index] = 0
                        start = pl.multiple_of(index * block, block)
                        pltpu.make_async_copy(
                            targets.at[pl.ds(start, block), :], packed.at[place], sems.at[place]
                        ).start()

                    @pl.when(jnp.logical_not(giving))
                    def _():
                        slots[place] = target_count + index
                        masks[target_count + index] = mask

            return carry

        lax.fori_loop(0, target_count, consider, 0)

    offer(False)
    offer(True)
    count = jnp.int32(0)
    union = jnp.int32(0)
    for index in range(target_count):
        mask = both[mine * target_count + index]
        masks[index] = mask
        listed[count] = index
        count = count + jnp.where(mask != 0, 1, 0)
        union = union | mask
    own = count
    foreign = jnp.where(giving, 0, state[0])

    def append(place, gathered):
        index = slots[place]
        listed[own + place] = index
        return gathered | masks[index]

    union = lax.fori_loop(0, foreign, append, union)
    meta[0] = own
    meta[1] = own + foreign
    meta[2] = union

    def finish(place, carry):
        pltpu.make_async_copy(
            targets.at[pl.ds(0, block), :], packed.at[place], sems.at[place]
        ).wait()
        return carry

    lax.fori_loop(0, jnp.where(giving, state[0], 0), finish, 0)


def plan(pair_targets, pair_counts, rank, targets, block):
    total = 2 * (targets.shape[0] // block)
    cap = min(moved_cap, total // 2)
    smem = pl.BlockSpec(memory_space=pltpu.SMEM)
    table = jax.ShapeDtypeStruct((total + 1,), jnp.int32)
    return pl.pallas_call(
        plan_kernel,
        out_shape=(
            table, table, jax.ShapeDtypeStruct((8,), jnp.int32), table,
            jax.ShapeDtypeStruct((cap, block, targets.shape[1]), targets.dtype),
        ),
        in_specs=[smem, smem, smem, pl.BlockSpec(memory_space=pl.ANY)],
        out_specs=(smem, smem, smem, smem, pl.BlockSpec(memory_space=pltpu.VMEM)),
        scratch_shapes=[
            pltpu.SMEM((total + 1,), jnp.int32),
            pltpu.SMEM((cap,), jnp.int32),
            pltpu.SMEM((2,), jnp.int32),
            pltpu.SemaphoreType.DMA((cap,)),
        ],
        name="plan",
    )(pair_targets, pair_counts, rank, targets)


def squares_kernel(meta, named_blocks, points, out, buffer, sums, sems):
    pieces_per, lanes = out.shape[1:]
    block = pieces_per * lanes
    slots = buffer.shape[0]
    ones = jnp.ones((8, 2 * points.shape[1]), jnp.bfloat16)
    count = meta[3]

    def fetch(position):
        slot = lax.rem(position, slots)
        start = pl.multiple_of(named_blocks[position] * block, block)
        return pltpu.make_async_copy(
            points.at[pl.ds(start, block), :], buffer.at[slot], sems.at[slot]
        )

    def begin(position):
        @pl.when(position < count)
        def _():
            fetch(position).start()

    group = slots // 2
    for position in range(group):
        begin(jnp.int32(position))
    out[...] = jnp.zeros_like(out)

    def visit(turn, carry):
        first = turn * group
        for at in range(group):
            begin(first + group + at)
        for at in range(group):
            @pl.when(first + at < count)
            def _():
                fetch(first + at).wait()
        side = lax.rem(turn, 2) * group
        for at in range(group):
            wide = buffer[side + at].astype(jnp.float32)
            summed = lax.dot_general(
                ones, two_pieces(wide * wide), NT, preferred_element_type=jnp.float32
            )
            for h in range(pieces_per):
                sums[at, h : h + 1, :] = 0.5 * summed[0:1, h * lanes : (h + 1) * lanes]
        for at in range(group):
            @pl.when(first + at < count)
            def _():
                out[named_blocks[first + at]] = sums[at]
        return carry

    lax.fori_loop(0, (count + group - 1) // group, visit, 0)


def named_squares(meta, named_blocks, points, block):
    smem = pl.BlockSpec(memory_space=pltpu.SMEM)
    return pl.pallas_call(
        squares_kernel,
        out_shape=jax.ShapeDtypeStruct((points.shape[0] // block, block // 128, 128), jnp.float32),
        in_specs=[smem, smem, pl.BlockSpec(memory_space=pl.ANY)],
        out_specs=pl.BlockSpec(memory_space=pltpu.VMEM),
        scratch_shapes=[
            pltpu.VMEM((8, block, points.shape[1]), points.dtype),
            pltpu.VMEM((4, block // 128, 128), jnp.float32),
            pltpu.SemaphoreType.DMA((8,)),
        ],
        cost_estimate=pl.CostEstimate(
            flops=2 * points.size, bytes_accessed=2 * points.size, transcendentals=0
        ),
        name="squares",
    )(meta, named_blocks, points)


def half_squares(points):
    widened = points.astype(jnp.float32)
    return 0.5 * jnp.sum(widened * widened, axis=1)


def sweep_kernel(
    masks, listed, meta, stored, targets, foreign,
    row_pot, row_sq, col_pot, col_sq, far_pot, far_sq,
    row_out, col_out, far_out,
    points, near_block, next_block, near_bias, next_bias, features, row_acc, col_acc, col_sum, faults, slow_row, full, sems, point_sem,
):
    source_count, pieces_per, lanes = row_pot.shape
    target_count = col_pot.shape[0]
    block = pieces_per * lanes
    width = points.shape[1]
    own, active = meta[0], meta[1]

    blocks, biases = (near_block, next_block), (near_bias, next_bias)

    def start_fetch(position, slot):
        @pl.when(position < own)
        def _():
            start = pl.multiple_of(listed[position] * block, block)
            pltpu.make_async_copy(
                targets.at[pl.ds(start, block), :], blocks[slot], sems.at[slot]
            ).start()

        @pl.when((position >= own) & (position < active))
        def _():
            pltpu.make_async_copy(foreign.at[position - own], blocks[slot], sems.at[slot]).start()

    bring = pltpu.make_async_copy(stored, points, point_sem)
    bring.start()
    start_fetch(0, 0)

    for h in range(pieces_per):
        shifted = row_pot[:, h, :] - row_sq[:, h, :]
        parts = [part.astype(jnp.float32) for part in pieces(shifted)]
        ones = jnp.ones((3, lanes), jnp.float32)
        pad = jnp.zeros((width - 3 * source_count - 3, lanes), jnp.float32)
        turned = jnp.concatenate(parts + [ones, pad], axis=0).T
        features[h * lanes : (h + 1) * lanes, :] = turned.astype(jnp.bfloat16)
    tallest = jnp.maximum(jnp.max(col_pot[...]), jnp.max(far_pot[...]))
    offset = (jnp.max(row_pot[...]) + tallest) / epsilon - headroom
    row_acc[...] = jnp.zeros_like(row_acc)
    col_sum[...] = jnp.zeros_like(col_sum)
    faults[...] = jnp.zeros_like(faults)
    lane = lax.broadcasted_iota(jnp.int32, (1, width), 1)

    def pattern(source):
        chosen = (lax.rem(lane, source_count) == source) & (lane < 3 * source_count)
        return jnp.where(chosen, 1.0, 0.0).astype(jnp.bfloat16)

    def prepare(position, slot):
        target = listed[jnp.minimum(position, active - 1)]
        near = jnp.minimum(target, target_count - 1)
        far = jnp.maximum(target - target_count, 0)
        term = jnp.where(
            target < target_count, col_pot[near] - col_sq[near], far_pot[far] - far_sq[far]
        )
        parts = [part.astype(jnp.float32) for part in pieces(term - offset * epsilon)]
        before = jnp.zeros((3 * source_count, lanes), jnp.float32)
        after = jnp.zeros((width - 3 * source_count - 3, lanes), jnp.float32)
        for h in range(pieces_per):
            rows = [before] + [part[h : h + 1, :] for part in parts] + [after]
            turned = jnp.concatenate(rows, axis=0).T
            biases[slot][h * lanes : (h + 1) * lanes, :] = turned.astype(jnp.bfloat16)

    def right_side(slot, source, cols):
        extra = biases[slot][cols, :] + pattern(source)
        return jnp.concatenate([blocks[slot][cols, :], extra], axis=1)

    def fast_tile(position, slot, target, source):
        prepare(position + 1, 1 - slot)
        rows = pl.ds(pl.multiple_of(source * block, block), block)
        lhs = jnp.concatenate([points[rows, :], features[...]], axis=1)
        for c in range(block // 256):
            cols = slice(c * 256, (c + 1) * 256)
            s = lax.dot_general(
                lhs, right_side(slot, source, cols), NT, preferred_element_type=jnp.float32
            )
            e = jnp.exp2(s * (log2e / epsilon))
            row_acc[rows, :] += e[:, :128] + e[:, 128:]
            col_acc[:, cols] += jnp.sum(e.reshape(block // 8, 8, 256), axis=0)

    def fast_end(target):
        summed = jnp.sum(col_acc[...], axis=0, keepdims=True)
        safe = (summed > smallest) & (summed < largest)
        faults[0:1, :] = jnp.maximum(faults[0:1, :], jnp.where(safe, 0.0, 1.0))
        for h in range(pieces_per):
            col_sum[target, h : h + 1, :] = summed[:, h * lanes : (h + 1) * lanes]

    def slow_tile(position, slot, target, source):
        first_row = pl.multiple_of(source * block, block)
        full[8:16, :] = jnp.full((8, block), absent, jnp.float32)

        def logits(r):
            rows = pl.ds(pl.multiple_of(first_row + r * 128, 128), 128)
            near = pl.ds(pl.multiple_of(r * 128, 128), 128)
            lhs = jnp.concatenate([points[rows, :], features[near, :]], axis=1)
            made = []
            for c in range(block // 256):
                rhs = right_side(slot, source, slice(c * 256, (c + 1) * 256))
                made.append(lax.dot_general(lhs, rhs, NT, preferred_element_type=jnp.float32))
            return rows, jnp.concatenate(made, axis=1) * (1.0 / epsilon)

        def first_pass(r, carry):
            rows, t = logits(r)
            top = jnp.max(t, axis=1, keepdims=True)
            lse = top + jnp.log(jnp.sum(jnp.exp(t - top), axis=1, keepdims=True))
            slow_row[rows, :] = log_add(slow_row[rows, :], jnp.broadcast_to(lse, (128, width)))
            full[8:9, :] = jnp.maximum(full[8:9, :], jnp.max(t, axis=0, keepdims=True))
            return carry

        lax.fori_loop(0, block // 128, first_pass, 0)
        full[16:17, :] = jnp.zeros((1, block), jnp.float32)

        def second_pass(r, carry):
            rows, t = logits(r)
            full[16:17, :] += jnp.sum(jnp.exp(t - full[8:9, :]), axis=0, keepdims=True)
            return carry

        lax.fori_loop(0, block // 128, second_pass, 0)
        lse = full[8:9, :] + jnp.log(full[16:17, :])
        col_acc[0:1, :] = log_add(col_acc[0:1, :], lse)

    def slow_end(target):
        for h in range(pieces_per):
            col_sum[target, h : h + 1, :] = col_acc[0:1, h * lanes : (h + 1) * lanes]

    def over_pairs(tile, end, fast):
        def visit(position, slot):
            target = listed[position]
            fetch_wait(slot)
            start_fetch(position + 1, 1 - slot)
            if not fast:
                prepare(position, slot)
            col_acc[...] = jnp.full(col_acc.shape, 0.0 if fast else absent, jnp.float32)
            mask = masks[target]

            def each(source, inner):
                @pl.when(((mask >> source) & 1) == 1)
                def _():
                    tile(position, slot, target, source)

                return inner

            lax.fori_loop(0, source_count, each, 0)
            end(target)

        def two_visits(turn, carry):
            visit(2 * turn, 0)

            @pl.when(2 * turn + 1 < active)
            def _():
                visit(2 * turn + 1, 1)

            return carry

        lax.fori_loop(0, (active + 1) // 2, two_visits, 0)

    def fetch_wait(slot):
        pltpu.make_async_copy(targets.at[pl.ds(0, block), :], blocks[slot], sems.at[slot]).wait()

    bring.wait()

    @pl.when(active > 0)
    def _():
        prepare(0, 0)

    over_pairs(fast_tile, fast_end, True)

    def put_rows(source, row):
        for h in range(pieces_per):
            row_out[source, h : h + 1, :] = row[:, h * lanes : (h + 1) * lanes]

    for source in range(source_count):
        summed = lane_sums(row_acc[source * block : (source + 1) * block, :])
        wanted = ((meta[2] >> source) & 1) == 1
        safe = ((summed > smallest) & (summed < largest)) | jnp.logical_not(wanted)
        faults[0:1, :] = jnp.maximum(faults[0:1, :], jnp.where(safe, 0.0, 1.0))
        put_rows(source, jnp.where(summed > 0, jnp.log(summed) + offset, absent))
    sums = col_sum[...]
    made = jnp.where(sums > 0, jnp.log(sums) + offset, absent)
    col_out[...] = made[:target_count]
    far_out[...] = made[target_count:]

    @pl.when(jnp.max(faults[0:1, :]) > 0)
    def _():
        slow_row[...] = jnp.full(slow_row.shape, absent, jnp.float32)
        col_sum[...] = jnp.full(col_sum.shape, absent, jnp.float32)
        start_fetch(0, 0)
        over_pairs(slow_tile, slow_end, False)
        col_out[...] = col_sum[:target_count] + offset
        far_out[...] = col_sum[target_count:] + offset
        for source in range(source_count):
            put_rows(source, lane_first(slow_row[source * block : (source + 1) * block, :]) + offset)


def sweep(masks, listed, meta, points, targets, foreign, *cells):
    row_pot, col_pot = cells[0], cells[2]
    source_count, pieces_per, lanes = row_pot.shape
    target_count = col_pot.shape[0]
    block = pieces_per * lanes
    width = points.shape[1]
    vmem = pl.BlockSpec(memory_space=pltpu.VMEM)
    smem = pl.BlockSpec(memory_space=pltpu.SMEM)
    anywhere = pl.BlockSpec(memory_space=pl.ANY)
    rows = jax.ShapeDtypeStruct(row_pot.shape, jnp.float32)
    cols = jax.ShapeDtypeStruct(col_pot.shape, jnp.float32)
    pairs = 3 * source_count
    return pl.pallas_call(
        sweep_kernel,
        out_shape=(rows, cols, cols),
        in_specs=[smem, smem, smem, anywhere, anywhere, anywhere] + [vmem] * len(cells),
        out_specs=(vmem, vmem, vmem),
        scratch_shapes=[
            pltpu.VMEM(points.shape, points.dtype),
            pltpu.VMEM((block, width), jnp.bfloat16),
            pltpu.VMEM((block, width), jnp.bfloat16),
            pltpu.VMEM((block, width), jnp.bfloat16),
            pltpu.VMEM((block, width), jnp.bfloat16),
            pltpu.VMEM((block, width), jnp.bfloat16),
            pltpu.VMEM((source_count * block, width), jnp.float32),
            pltpu.VMEM((8, block), jnp.float32),
            pltpu.VMEM((2 * target_count, pieces_per, lanes), jnp.float32),
            pltpu.VMEM((8, block), jnp.float32),
            pltpu.VMEM((source_count * block, width), jnp.float32),
            pltpu.VMEM((24, block), jnp.float32),
            pltpu.SemaphoreType.DMA((2,)),
            pltpu.SemaphoreType.DMA,
        ],
        compiler_params=pltpu.CompilerParams(vmem_limit_bytes=40 * 1024 * 1024),
        cost_estimate=pl.CostEstimate(
            flops=2 * pairs * block * block * width,
            bytes_accessed=pairs * block * width * 2,
            transcendentals=pairs * block * block,
        ),
        name="sweep",
    )(masks, listed, meta, points, targets, foreign, *cells)


def swapped(value, axis, size, step):
    return lax.ppermute(value, axis, [(i, i ^ step) for i in range(size)])


def exchange(value, axis, size):
    if size == 1:
        return value
    half = value.shape[0] // 2
    low = lax.rem(lax.axis_index(axis), 2)
    kept = lax.dynamic_slice_in_dim(value, low * half, half, 0)
    sent = lax.dynamic_slice_in_dim(value, (1 - low) * half, half, 0)
    kept = log_add(kept, swapped(sent, axis, size, 1))
    step = 2
    while step < size:
        kept = log_add(kept, swapped(kept, axis, size, step))
        step *= 2
    other = swapped(kept, axis, size, 1)
    return jnp.where(
        low == 0, jnp.concatenate([kept, other], axis=0), jnp.concatenate([other, kept], axis=0)
    )


def doubled(value, axis, size):
    step = 1
    while step < size:
        value = log_add(value, swapped(value, axis, size, step))
        step *= 2
    return value


def local(
    source_points, target_points, source_potential, target_potential,
    source_log_mass, target_log_mass, pair_targets, pair_counts,
):
    source_count = pair_targets.shape[0]
    block = source_points.shape[0] // source_count
    src_size, tgt_size = lax.axis_size("src"), lax.axis_size("tgt")
    rank = lax.axis_index("tgt").astype(jnp.int32).reshape(1)

    def by_block(value):
        return value.reshape(-1, block // 128, 128)

    masks, listed, meta, named_blocks, packed = plan(pair_targets, pair_counts, rank, target_points, block)
    foreign = swapped(packed, "tgt", tgt_size, 1)
    row_pot, col_pot = by_block(source_potential), by_block(target_potential)
    row_mass, col_mass = by_block(source_log_mass), by_block(target_log_mass)
    row_sq = by_block(half_squares(source_points))
    col_sq = named_squares(meta, named_blocks, target_points, block)
    far_sq = swapped(col_sq, "tgt", tgt_size, 1)
    for _ in range(ITERS):
        far_pot = swapped(col_pot, "tgt", tgt_size, 1)
        rows, cols, far = sweep(
            masks, listed, meta, source_points, target_points, foreign,
            row_pot, row_sq, col_pot, col_sq, far_pot, far_sq,
        )
        cols = log_add(cols, swapped(far, "tgt", tgt_size, 1))
        rows = doubled(rows, "tgt", tgt_size)
        cols = exchange(cols, "src", src_size)
        row_pot = row_pot + (0.5 * epsilon) * (row_mass - rows)
        col_pot = col_pot + (0.5 * epsilon) * (col_mass - cols)
    return row_pot.reshape(-1), col_pot.reshape(-1)


def solution(mesh):
    placed = (
        P("src", None), P("tgt", None), P("src"), P("tgt"),
        P("src"), P("tgt"), P("src", None), P("src"),
    )
    return jax.shard_map(
        local, mesh=mesh, in_specs=placed, out_specs=(P("src"), P("tgt")), check_vma=False
    )
```

```python
import functools
import jax
import jax.numpy as jnp
from jax import lax
from jax.experimental import pallas as pl
from jax.experimental.pallas import tpu as pltpu
from jax.sharding import PartitionSpec as P

ITERS = 2
moved_cap = 8
epsilon = 0.5
absent = -1e30
log2e = 1.4426950408889634
headroom = 60.0
smallest = 1e-26
largest = 1e37
NT = (((1,), (1,)), ((), ()))


def pieces(value):
    high = value.astype(jnp.bfloat16)
    rest = value - high.astype(jnp.float32)
    middle = rest.astype(jnp.bfloat16)
    low = (rest - middle.astype(jnp.float32)).astype(jnp.bfloat16)
    return high, middle, low


def lane_sums(block):
    return jnp.sum(block.T, axis=0, keepdims=True)


def two_pieces(value):
    high = value.astype(jnp.bfloat16)
    low = (value - high.astype(jnp.float32)).astype(jnp.bfloat16)
    return jnp.concatenate([high, low], axis=1)


def lane_first(block):
    lane = lax.broadcasted_iota(jnp.int32, (8, block.shape[1]), 1)
    pick = jnp.where(lane == 0, 1.0, 0.0).astype(jnp.bfloat16)
    total = None
    for part in pieces(block):
        product = lax.dot_general(pick, part, NT, preferred_element_type=jnp.float32)
        total = product if total is None else total + product
    return total[0:1]


def log_add(first, second):
    top = jnp.maximum(first, second)
    return top + jnp.log(jnp.exp(first - top) + jnp.exp(second - top))


def bit_count(value):
    value = value - ((value >> 1) & 0x55555555)
    value = (value & 0x33333333) + ((value >> 2) & 0x33333333)
    value = (value + (value >> 4)) & 0x0F0F0F0F
    return (value * 0x01010101) >> 24


def plan_kernel(
    pair_targets, pair_counts, rank, targets,
    masks, listed, meta, named_blocks, packed,
    both, slots, state, sems,
):
    source_count, slot_width = pair_targets.shape
    total = both.shape[0] - 1
    target_count = total // 2
    block = packed.shape[1]
    mine = lax.rem(rank[0], 2)
    base = (rank[0] - mine) * target_count
    for index in range(total + 1):
        both[index] = 0
    low_load = jnp.int32(0)
    high_load = jnp.int32(0)
    for source in range(source_count):
        count = pair_counts[source]
        for slot in range(slot_width):
            place = pair_targets[source, slot] - base
            here = (slot < count) & (place >= 0) & (place < total)
            index = jnp.where(here, place, total)
            both[index] = both[index] | (1 << source)
            low_load = low_load + jnp.where(here & (place < target_count), 1, 0)
            high_load = high_load + jnp.where(here & (place >= target_count), 1, 0)
    named = jnp.int32(0)
    for index in range(target_count):
        named_blocks[named] = index
        named = named + jnp.where(both[mine * target_count + index] != 0, 1, 0)
    meta[3] = named
    heavy = jnp.where(high_load > low_load, 1, 0)
    wanted = jnp.abs(high_load - low_load) // 2
    state[0] = 0
    state[1] = 0
    first = heavy * target_count
    giving = mine == heavy

    def offer(single):
        def consider(index, carry):
            mask = both[first + index]
            rest = mask & (mask - 1)
            apt = ((mask != 0) & (rest == 0)) if single else (rest != 0)

            @pl.when(apt & (state[0] < packed.shape[0]))
            def _():
                count = 1 if single else bit_count(mask)

                @pl.when(state[1] + count <= wanted)
                def _():
                    place = state[0]
                    state[0] = place + 1
                    state[1] = state[1] + count

                    @pl.when(giving)
                    def _():
                        both[first + index] = 0
                        start = pl.multiple_of(index * block, block)
                        pltpu.make_async_copy(
                            targets.at[pl.ds(start, block), :], packed.at[place], sems.at[place]
                        ).start()

                    @pl.when(jnp.logical_not(giving))
                    def _():
                        slots[place] = target_count + index
                        masks[target_count + index] = mask

            return carry

        lax.fori_loop(0, target_count, consider, 0)

    offer(False)
    offer(True)
    count = jnp.int32(0)
    union = jnp.int32(0)
    for index in range(target_count):
        mask = both[mine * target_count + index]
        masks[index] = mask
        listed[count] = index
        count = count + jnp.where(mask != 0, 1, 0)
        union = union | mask
    own = count
    foreign = jnp.where(giving, 0, state[0])

    def append(place, gathered):
        index = slots[place]
        listed[own + place] = index
        return gathered | masks[index]

    union = lax.fori_loop(0, foreign, append, union)
    meta[0] = own
    meta[1] = own + foreign
    meta[2] = union

    def finish(place, carry):
        pltpu.make_async_copy(
            targets.at[pl.ds(0, block), :], packed.at[place], sems.at[place]
        ).wait()
        return carry

    lax.fori_loop(0, jnp.where(giving, state[0], 0), finish, 0)


def plan(pair_targets, pair_counts, rank, targets, block):
    total = 2 * (targets.shape[0] // block)
    cap = min(moved_cap, total // 2)
    smem = pl.BlockSpec(memory_space=pltpu.SMEM)
    table = jax.ShapeDtypeStruct((total + 1,), jnp.int32)
    return pl.pallas_call(
        plan_kernel,
        out_shape=(
            table, table, jax.ShapeDtypeStruct((8,), jnp.int32), table,
            jax.ShapeDtypeStruct((cap, block, targets.shape[1]), targets.dtype),
        ),
        in_specs=[smem, smem, smem, pl.BlockSpec(memory_space=pl.ANY)],
        out_specs=(smem, smem, smem, smem, pl.BlockSpec(memory_space=pltpu.VMEM)),
        scratch_shapes=[
            pltpu.SMEM((total + 1,), jnp.int32),
            pltpu.SMEM((cap,), jnp.int32),
            pltpu.SMEM((2,), jnp.int32),
            pltpu.SemaphoreType.DMA((cap,)),
        ],
        name="plan",
    )(pair_targets, pair_counts, rank, targets)


def squares_kernel(meta, named_blocks, points, out, buffer, sums, sems):
    pieces_per, lanes = out.shape[1:]
    block = pieces_per * lanes
    slots = buffer.shape[0]
    ones = jnp.ones((8, 2 * points.shape[1]), jnp.bfloat16)
    count = meta[3]

    def fetch(position):
        slot = lax.rem(position, slots)
        start = pl.multiple_of(named_blocks[position] * block, block)
        return pltpu.make_async_copy(
            points.at[pl.ds(start, block), :], buffer.at[slot], sems.at[slot]
        )

    def begin(position):
        @pl.when(position < count)
        def _():
            fetch(position).start()

    group = sums.shape[0]
    for position in range(slots - group):
        begin(jnp.int32(position))
    out[...] = jnp.zeros_like(out)

    def visit(turn, carry):
        first = turn * group
        for at in range(group):
            begin(first + slots - group + at)
        for at in range(group):
            @pl.when(first + at < count)
            def _():
                fetch(first + at).wait()
        side = lax.rem(first, slots)
        for at in range(group):
            wide = buffer[side + at].astype(jnp.float32)
            square = wide * wide
            if at % 2 == 0:
                summed = lax.dot_general(
                    ones, two_pieces(square), NT, preferred_element_type=jnp.float32
                )
            for h in range(pieces_per):
                part = slice(h * lanes, (h + 1) * lanes)
                row = summed[0:1, part] if at % 2 == 0 else lane_sums(square[part, :])
                sums[at, h : h + 1, :] = 0.5 * row
        for at in range(group):
            @pl.when(first + at < count)
            def _():
                out[named_blocks[first + at]] = sums[at]
        return carry

    lax.fori_loop(0, (count + group - 1) // group, visit, 0)


def named_squares(meta, named_blocks, points, block):
    smem = pl.BlockSpec(memory_space=pltpu.SMEM)
    return pl.pallas_call(
        squares_kernel,
        out_shape=jax.ShapeDtypeStruct((points.shape[0] // block, block // 128, 128), jnp.float32),
        in_specs=[smem, smem, pl.BlockSpec(memory_space=pl.ANY)],
        out_specs=pl.BlockSpec(memory_space=pltpu.VMEM),
        scratch_shapes=[
            pltpu.VMEM((16, block, points.shape[1]), points.dtype),
            pltpu.VMEM((4, block // 128, 128), jnp.float32),
            pltpu.SemaphoreType.DMA((16,)),
        ],
        cost_estimate=pl.CostEstimate(
            flops=2 * points.size, bytes_accessed=2 * points.size, transcendentals=0
        ),
        name="squares",
    )(meta, named_blocks, points)


def half_squares(points):
    widened = points.astype(jnp.float32)
    return 0.5 * jnp.sum(widened * widened, axis=1)


def sweep_kernel(
    masks, listed, meta, stored, targets, foreign,
    row_pot, row_sq, col_pot, col_sq, far_pot, far_sq,
    row_out, col_out, far_out,
    points, blocks, near_bias, next_bias, features, row_acc, col_acc, col_sum, faults, slow_row, full, sems, point_sem,
):
    source_count, pieces_per, lanes = row_pot.shape
    target_count = col_pot.shape[0]
    block = pieces_per * lanes
    width = points.shape[1]
    own, active = meta[0], meta[1]

    biases = (near_bias, next_bias)
    ring = blocks.shape[0]

    def start_fetch(position):
        slot = lax.rem(position, ring)

        @pl.when(position < own)
        def _():
            start = pl.multiple_of(listed[position] * block, block)
            pltpu.make_async_copy(
                targets.at[pl.ds(start, block), :], blocks.at[slot], sems.at[slot]
            ).start()

        @pl.when((position >= own) & (position < active))
        def _():
            pltpu.make_async_copy(
                foreign.at[position - own], blocks.at[slot], sems.at[slot]
            ).start()

    bring = pltpu.make_async_copy(stored, points, point_sem)
    bring.start()
    for ahead in range(ring - 1):
        start_fetch(jnp.int32(ahead))

    for h in range(pieces_per):
        shifted = row_pot[:, h, :] - row_sq[:, h, :]
        parts = [part.astype(jnp.float32) for part in pieces(shifted)]
        ones = jnp.ones((3, lanes), jnp.float32)
        pad = jnp.zeros((width - 3 * source_count - 3, lanes), jnp.float32)
        turned = jnp.concatenate(parts + [ones, pad], axis=0).T
        features[h * lanes : (h + 1) * lanes, :] = turned.astype(jnp.bfloat16)
    tallest = jnp.maximum(jnp.max(col_pot[...]), jnp.max(far_pot[...]))
    offset = (jnp.max(row_pot[...]) + tallest) / epsilon - headroom
    row_acc[...] = jnp.zeros_like(row_acc)
    col_sum[...] = jnp.zeros_like(col_sum)
    faults[...] = jnp.zeros_like(faults)
    lane = lax.broadcasted_iota(jnp.int32, (1, width), 1)

    def pattern(source):
        chosen = (lax.rem(lane, source_count) == source) & (lane < 3 * source_count)
        return jnp.where(chosen, 1.0, 0.0).astype(jnp.bfloat16)

    def prepare(position, slot):
        target = listed[jnp.minimum(position, active - 1)]
        near = jnp.minimum(target, target_count - 1)
        far = jnp.maximum(target - target_count, 0)
        term = jnp.where(
            target < target_count, col_pot[near] - col_sq[near], far_pot[far] - far_sq[far]
        )
        parts = [part.astype(jnp.float32) for part in pieces(term - offset * epsilon)]
        before = jnp.zeros((3 * source_count, lanes), jnp.float32)
        after = jnp.zeros((width - 3 * source_count - 3, lanes), jnp.float32)
        for h in range(pieces_per):
            rows = [before] + [part[h : h + 1, :] for part in parts] + [after]
            turned = jnp.concatenate(rows, axis=0).T
            biases[slot][h * lanes : (h + 1) * lanes, :] = turned.astype(jnp.bfloat16)

    def right_side(position, slot, source, cols):
        extra = biases[slot][cols, :] + pattern(source)
        return jnp.concatenate([blocks[lax.rem(position, ring), cols, :], extra], axis=1)

    def fast_tile(position, slot, target, source):
        prepare(position + 1, 1 - slot)
        rows = pl.ds(pl.multiple_of(source * block, block), block)
        lhs = jnp.concatenate([points[rows, :], features[...]], axis=1)
        for c in range(block // 256):
            cols = slice(c * 256, (c + 1) * 256)
            s = lax.dot_general(
                lhs, right_side(position, slot, source, cols), NT, preferred_element_type=jnp.float32
            )
            e = jnp.exp2(s * (log2e / epsilon))
            row_acc[rows, :] += e[:, :128] + e[:, 128:]
            col_acc[:, cols] += jnp.sum(e.reshape(block // 8, 8, 256), axis=0)

    def fast_end(target):
        summed = jnp.sum(col_acc[...], axis=0, keepdims=True)
        safe = (summed > smallest) & (summed < largest)
        faults[0:1, :] = jnp.maximum(faults[0:1, :], jnp.where(safe, 0.0, 1.0))
        for h in range(pieces_per):
            col_sum[target, h : h + 1, :] = summed[:, h * lanes : (h + 1) * lanes]

    def slow_tile(position, slot, target, source):
        first_row = pl.multiple_of(source * block, block)
        full[8:16, :] = jnp.full((8, block), absent, jnp.float32)

        def logits(r):
            rows = pl.ds(pl.multiple_of(first_row + r * 128, 128), 128)
            near = pl.ds(pl.multiple_of(r * 128, 128), 128)
            lhs = jnp.concatenate([points[rows, :], features[near, :]], axis=1)
            made = []
            for c in range(block // 256):
                rhs = right_side(position, slot, source, slice(c * 256, (c + 1) * 256))
                made.append(lax.dot_general(lhs, rhs, NT, preferred_element_type=jnp.float32))
            return rows, jnp.concatenate(made, axis=1) * (1.0 / epsilon)

        def first_pass(r, carry):
            rows, t = logits(r)
            top = jnp.max(t, axis=1, keepdims=True)
            lse = top + jnp.log(jnp.sum(jnp.exp(t - top), axis=1, keepdims=True))
            slow_row[rows, :] = log_add(slow_row[rows, :], jnp.broadcast_to(lse, (128, width)))
            full[8:9, :] = jnp.maximum(full[8:9, :], jnp.max(t, axis=0, keepdims=True))
            return carry

        lax.fori_loop(0, block // 128, first_pass, 0)
        full[16:17, :] = jnp.zeros((1, block), jnp.float32)

        def second_pass(r, carry):
            rows, t = logits(r)
            full[16:17, :] += jnp.sum(jnp.exp(t - full[8:9, :]), axis=0, keepdims=True)
            return carry

        lax.fori_loop(0, block // 128, second_pass, 0)
        lse = full[8:9, :] + jnp.log(full[16:17, :])
        col_acc[0:1, :] = log_add(col_acc[0:1, :], lse)

    def slow_end(target):
        for h in range(pieces_per):
            col_sum[target, h : h + 1, :] = col_acc[0:1, h * lanes : (h + 1) * lanes]

    def over_pairs(tile, end, fast):
        def visit(position, slot):
            target = listed[position]
            fetch_wait(position)
            start_fetch(position + ring - 1)
            if not fast:
                prepare(position, slot)
            col_acc[...] = jnp.full(col_acc.shape, 0.0 if fast else absent, jnp.float32)
            mask = masks[target]

            def each(_, left):
                lowest = left & -left
                tile(position, slot, target, bit_count(lowest - 1))
                return left - lowest

            lax.fori_loop(0, bit_count(mask), each, mask)
            end(target)

        def two_visits(turn, carry):
            visit(2 * turn, 0)

            @pl.when(2 * turn + 1 < active)
            def _():
                visit(2 * turn + 1, 1)

            return carry

        lax.fori_loop(0, (active + 1) // 2, two_visits, 0)

    def fetch_wait(position):
        slot = lax.rem(position, ring)
        pltpu.make_async_copy(
            targets.at[pl.ds(0, block), :], blocks.at[slot], sems.at[slot]
        ).wait()

    bring.wait()

    @pl.when(active > 0)
    def _():
        prepare(0, 0)

    over_pairs(fast_tile, fast_end, True)

    def put_rows(source, row):
        for h in range(pieces_per):
            row_out[source, h : h + 1, :] = row[:, h * lanes : (h + 1) * lanes]

    for source in range(source_count):
        first_row = source * block
        summed = jnp.concatenate(
            [
                lane_sums(row_acc[first_row + h * lanes : first_row + (h + 1) * lanes, :])
                for h in range(pieces_per)
            ],
            axis=1,
        )
        wanted = ((meta[2] >> source) & 1) == 1
        safe = ((summed > smallest) & (summed < largest)) | jnp.logical_not(wanted)
        faults[0:1, :] = jnp.maximum(faults[0:1, :], jnp.where(safe, 0.0, 1.0))
        put_rows(source, jnp.where(summed > 0, jnp.log(summed) + offset, absent))
    sums = col_sum[...]
    made = jnp.where(sums > 0, jnp.log(sums) + offset, absent)
    col_out[...] = made[:target_count]
    far_out[...] = made[target_count:]

    @pl.when(jnp.max(faults[0:1, :]) > 0)
    def _():
        slow_row[...] = jnp.full(slow_row.shape, absent, jnp.float32)
        col_sum[...] = jnp.full(col_sum.shape, absent, jnp.float32)
        for ahead in range(ring - 1):
            start_fetch(jnp.int32(ahead))
        over_pairs(slow_tile, slow_end, False)
        col_out[...] = col_sum[:target_count] + offset
        far_out[...] = col_sum[target_count:] + offset
        for source in range(source_count):
            put_rows(source, lane_first(slow_row[source * block : (source + 1) * block, :]) + offset)


def sweep(masks, listed, meta, points, targets, foreign, *cells):
    row_pot, col_pot = cells[0], cells[2]
    source_count, pieces_per, lanes = row_pot.shape
    target_count = col_pot.shape[0]
    block = pieces_per * lanes
    width = points.shape[1]
    vmem = pl.BlockSpec(memory_space=pltpu.VMEM)
    smem = pl.BlockSpec(memory_space=pltpu.SMEM)
    anywhere = pl.BlockSpec(memory_space=pl.ANY)
    rows = jax.ShapeDtypeStruct(row_pot.shape, jnp.float32)
    cols = jax.ShapeDtypeStruct(col_pot.shape, jnp.float32)
    pairs = 3 * source_count
    return pl.pallas_call(
        sweep_kernel,
        out_shape=(rows, cols, cols),
        in_specs=[smem, smem, smem, anywhere, anywhere, anywhere] + [vmem] * len(cells),
        out_specs=(vmem, vmem, vmem),
        scratch_shapes=[
            pltpu.VMEM(points.shape, points.dtype),
            pltpu.VMEM((4, block, width), jnp.bfloat16),
            pltpu.VMEM((block, width), jnp.bfloat16),
            pltpu.VMEM((block, width), jnp.bfloat16),
            pltpu.VMEM((block, width), jnp.bfloat16),
            pltpu.VMEM((source_count * block, width), jnp.float32),
            pltpu.VMEM((8, block), jnp.float32),
            pltpu.VMEM((2 * target_count, pieces_per, lanes), jnp.float32),
            pltpu.VMEM((8, block), jnp.float32),
            pltpu.VMEM((source_count * block, width), jnp.float32),
            pltpu.VMEM((24, block), jnp.float32),
            pltpu.SemaphoreType.DMA((4,)),
            pltpu.SemaphoreType.DMA,
        ],
        compiler_params=pltpu.CompilerParams(vmem_limit_bytes=40 * 1024 * 1024),
        cost_estimate=pl.CostEstimate(
            flops=2 * pairs * block * block * width,
            bytes_accessed=pairs * block * width * 2,
            transcendentals=pairs * block * block,
        ),
        name="sweep",
    )(masks, listed, meta, points, targets, foreign, *cells)


def swapped(value, axis, size, step):
    return lax.ppermute(value, axis, [(i, i ^ step) for i in range(size)])


def exchange(value, axis, size, other_axis, other_size):
    steps = []
    while 2 ** len(steps) < size:
        steps.append(2 ** len(steps))
    if not steps:
        return value
    orders = [steps, steps[1:] + steps[:1]]

    def swap(sent, turn):
        pairs = [
            (i * other_size + k, (i ^ orders[k % 2][turn]) * other_size + k)
            for i in range(size)
            for k in range(other_size)
        ]
        return lax.ppermute(sent, (axis, other_axis), pairs)

    half = value.shape[0] // 2
    odd = lax.rem(lax.axis_index(other_axis), 2) == 1
    me = lax.axis_index(axis)
    low = jnp.where(odd, lax.rem(me // orders[1][0], 2), lax.rem(me // orders[0][0], 2))
    kept = lax.dynamic_slice_in_dim(value, low * half, half, 0)
    sent = lax.dynamic_slice_in_dim(value, (1 - low) * half, half, 0)
    kept = log_add(kept, swap(sent, 0))
    for turn in range(1, len(steps)):
        kept = log_add(kept, swap(kept, turn))
    other = swap(kept, 0)
    return jnp.where(
        low == 0, jnp.concatenate([kept, other], axis=0), jnp.concatenate([other, kept], axis=0)
    )


def doubled(value, axis, size):
    step = 1
    while step < size:
        value = log_add(value, swapped(value, axis, size, step))
        step *= 2
    return value


def local(
    source_points, target_points, source_potential, target_potential,
    source_log_mass, target_log_mass, pair_targets, pair_counts,
):
    source_count = pair_targets.shape[0]
    block = source_points.shape[0] // source_count
    src_size, tgt_size = lax.axis_size("src"), lax.axis_size("tgt")
    rank = lax.axis_index("tgt").astype(jnp.int32).reshape(1)

    def by_block(value):
        return value.reshape(-1, block // 128, 128)

    masks, listed, meta, named_blocks, packed = plan(pair_targets, pair_counts, rank, target_points, block)
    foreign = swapped(packed, "tgt", tgt_size, 1)
    row_pot, col_pot = by_block(source_potential), by_block(target_potential)
    row_mass, col_mass = by_block(source_log_mass), by_block(target_log_mass)
    row_sq = by_block(half_squares(source_points))
    col_sq = named_squares(meta, named_blocks, target_points, block)
    far_sq = swapped(col_sq, "tgt", tgt_size, 1)
    for _ in range(ITERS):
        far_pot = swapped(col_pot, "tgt", tgt_size, 1)
        rows, cols, far = sweep(
            masks, listed, meta, source_points, target_points, foreign,
            row_pot, row_sq, col_pot, col_sq, far_pot, far_sq,
        )
        cols = log_add(cols, swapped(far, "tgt", tgt_size, 1))
        rows = doubled(rows, "tgt", tgt_size)
        cols = exchange(cols, "src", src_size, "tgt", tgt_size)
        row_pot = row_pot + (0.5 * epsilon) * (row_mass - rows)
        col_pot = col_pot + (0.5 * epsilon) * (col_mass - cols)
    return row_pot.reshape(-1), col_pot.reshape(-1)


def solution(mesh):
    placed = (
        P("src", None), P("tgt", None), P("src"), P("tgt"),
        P("src"), P("tgt"), P("src", None), P("src"),
    )
    return jax.shard_map(
        local, mesh=mesh, in_specs=placed, out_specs=(P("src"), P("tgt")), check_vma=False
    )
```

```python
import functools
import jax
import jax.numpy as jnp
from jax import lax
from jax.experimental import pallas as pl
from jax.experimental.pallas import tpu as pltpu
from jax.sharding import PartitionSpec as P

ITERS = 2
moved_cap = 8
epsilon = 0.5
absent = -1e30
log2e = 1.4426950408889634
headroom = 60.0
smallest = 1e-26
largest = 1e37
NT = (((1,), (1,)), ((), ()))


def pieces(value):
    high = value.astype(jnp.bfloat16)
    rest = value - high.astype(jnp.float32)
    middle = rest.astype(jnp.bfloat16)
    low = (rest - middle.astype(jnp.float32)).astype(jnp.bfloat16)
    return high, middle, low


def lane_sums(block):
    return jnp.sum(block.T, axis=0, keepdims=True)


def two_pieces(value):
    high = value.astype(jnp.bfloat16)
    low = (value - high.astype(jnp.float32)).astype(jnp.bfloat16)
    return jnp.concatenate([high, low], axis=1)


def lane_first(block):
    lane = lax.broadcasted_iota(jnp.int32, (8, block.shape[1]), 1)
    pick = jnp.where(lane == 0, 1.0, 0.0).astype(jnp.bfloat16)
    total = None
    for part in pieces(block):
        product = lax.dot_general(pick, part, NT, preferred_element_type=jnp.float32)
        total = product if total is None else total + product
    return total[0:1]


def log_add(first, second):
    top = jnp.maximum(first, second)
    return top + jnp.log(jnp.exp(first - top) + jnp.exp(second - top))


def bit_count(value):
    value = value - ((value >> 1) & 0x55555555)
    value = (value & 0x33333333) + ((value >> 2) & 0x33333333)
    value = (value + (value >> 4)) & 0x0F0F0F0F
    return (value * 0x01010101) >> 24


def plan_kernel(
    pair_targets, pair_counts, rank, targets,
    masks, listed, meta, named_blocks, packed,
    both, slots, state, sems,
):
    source_count, slot_width = pair_targets.shape
    total = both.shape[0] - 1
    target_count = total // 2
    block = packed.shape[1]
    mine = lax.rem(rank[0], 2)
    base = (rank[0] - mine) * target_count
    for index in range(total + 1):
        both[index] = 0
    low_load = jnp.int32(0)
    high_load = jnp.int32(0)
    for source in range(source_count):
        count = pair_counts[source]
        for slot in range(slot_width):
            place = pair_targets[source, slot] - base
            here = (slot < count) & (place >= 0) & (place < total)
            index = jnp.where(here, place, total)
            both[index] = both[index] | (1 << source)
            low_load = low_load + jnp.where(here & (place < target_count), 1, 0)
            high_load = high_load + jnp.where(here & (place >= target_count), 1, 0)
    named = jnp.int32(0)
    for index in range(target_count):
        named_blocks[named] = index
        named = named + jnp.where(both[mine * target_count + index] != 0, 1, 0)
    meta[3] = named
    heavy = jnp.where(high_load > low_load, 1, 0)
    wanted = jnp.abs(high_load - low_load) // 2
    state[0] = 0
    state[1] = 0
    first = heavy * target_count
    giving = mine == heavy

    def offer(single):
        def consider(index, carry):
            mask = both[first + index]
            rest = mask & (mask - 1)
            apt = ((mask != 0) & (rest == 0)) if single else (rest != 0)

            @pl.when(apt & (state[0] < packed.shape[0]))
            def _():
                count = 1 if single else bit_count(mask)

                @pl.when(state[1] + count <= wanted)
                def _():
                    place = state[0]
                    state[0] = place + 1
                    state[1] = state[1] + count

                    @pl.when(giving)
                    def _():
                        both[first + index] = 0
                        start = pl.multiple_of(index * block, block)
                        pltpu.make_async_copy(
                            targets.at[pl.ds(start, block), :], packed.at[place], sems.at[place]
                        ).start()

                    @pl.when(jnp.logical_not(giving))
                    def _():
                        slots[place] = target_count + index
                        masks[target_count + index] = mask

            return carry

        lax.fori_loop(0, target_count, consider, 0)

    offer(False)
    offer(True)
    count = jnp.int32(0)
    union = jnp.int32(0)
    for index in range(target_count):
        mask = both[mine * target_count + index]
        masks[index] = mask
        listed[count] = index
        count = count + jnp.where(mask != 0, 1, 0)
        union = union | mask
    own = count
    foreign = jnp.where(giving, 0, state[0])

    def append(place, gathered):
        index = slots[place]
        listed[own + place] = index
        return gathered | masks[index]

    union = lax.fori_loop(0, foreign, append, union)
    meta[0] = own
    meta[1] = own + foreign
    meta[2] = union

    def finish(place, carry):
        pltpu.make_async_copy(
            targets.at[pl.ds(0, block), :], packed.at[place], sems.at[place]
        ).wait()
        return carry

    lax.fori_loop(0, jnp.where(giving, state[0], 0), finish, 0)


def plan(pair_targets, pair_counts, rank, targets, block):
    total = 2 * (targets.shape[0] // block)
    cap = min(moved_cap, total // 2)
    smem = pl.BlockSpec(memory_space=pltpu.SMEM)
    table = jax.ShapeDtypeStruct((total + 1,), jnp.int32)
    return pl.pallas_call(
        plan_kernel,
        out_shape=(
            table, table, jax.ShapeDtypeStruct((8,), jnp.int32), table,
            jax.ShapeDtypeStruct((cap, block, targets.shape[1]), targets.dtype),
        ),
        in_specs=[smem, smem, smem, pl.BlockSpec(memory_space=pl.ANY)],
        out_specs=(smem, smem, smem, smem, pl.BlockSpec(memory_space=pltpu.VMEM)),
        scratch_shapes=[
            pltpu.SMEM((total + 1,), jnp.int32),
            pltpu.SMEM((cap,), jnp.int32),
            pltpu.SMEM((2,), jnp.int32),
            pltpu.SemaphoreType.DMA((cap,)),
        ],
        name="plan",
    )(pair_targets, pair_counts, rank, targets)


def squares_kernel(meta, named_blocks, points, out, buffer, sums, sems):
    pieces_per, lanes = out.shape[1:]
    block = pieces_per * lanes
    slots = buffer.shape[0]
    ones = jnp.ones((8, 2 * points.shape[1]), jnp.bfloat16)
    count = meta[3]

    def fetch(position):
        slot = lax.rem(position, slots)
        start = pl.multiple_of(named_blocks[position] * block, block)
        return pltpu.make_async_copy(
            points.at[pl.ds(start, block), :], buffer.at[slot], sems.at[slot]
        )

    def begin(position):
        @pl.when(position < count)
        def _():
            fetch(position).start()

    group = sums.shape[0]
    for position in range(slots - group):
        begin(jnp.int32(position))
    out[...] = jnp.zeros_like(out)

    def visit(turn, carry):
        first = turn * group
        for at in range(group):
            begin(first + slots - group + at)
        for at in range(group):
            @pl.when(first + at < count)
            def _():
                fetch(first + at).wait()
        side = lax.rem(first, slots)
        for at in range(group):
            wide = buffer[side + at].astype(jnp.float32)
            square = wide * wide
            if at % 2 == 0:
                summed = lax.dot_general(
                    ones, two_pieces(square), NT, preferred_element_type=jnp.float32
                )
            for h in range(pieces_per):
                part = slice(h * lanes, (h + 1) * lanes)
                row = summed[0:1, part] if at % 2 == 0 else lane_sums(square[part, :])
                sums[at, h : h + 1, :] = 0.5 * row
        for at in range(group):
            @pl.when(first + at < count)
            def _():
                out[named_blocks[first + at]] = sums[at]
        return carry

    lax.fori_loop(0, (count + group - 1) // group, visit, 0)


def named_squares(meta, named_blocks, points, block):
    smem = pl.BlockSpec(memory_space=pltpu.SMEM)
    return pl.pallas_call(
        squares_kernel,
        out_shape=jax.ShapeDtypeStruct((points.shape[0] // block, block // 128, 128), jnp.float32),
        in_specs=[smem, smem, pl.BlockSpec(memory_space=pl.ANY)],
        out_specs=pl.BlockSpec(memory_space=pltpu.VMEM),
        scratch_shapes=[
            pltpu.VMEM((16, block, points.shape[1]), points.dtype),
            pltpu.VMEM((4, block // 128, 128), jnp.float32),
            pltpu.SemaphoreType.DMA((16,)),
        ],
        cost_estimate=pl.CostEstimate(
            flops=2 * points.size, bytes_accessed=2 * points.size, transcendentals=0
        ),
        name="squares",
    )(meta, named_blocks, points)


def half_squares(points):
    widened = points.astype(jnp.float32)
    return 0.5 * jnp.sum(widened * widened, axis=1)


def sweep_kernel(
    masks, listed, meta, stored, targets, foreign,
    row_pot, row_sq, col_pot, col_sq, far_pot, far_sq,
    row_out, col_out, far_out,
    points, blocks, bias_a, bias_b, bias_c, bias_d, features, row_acc, row_too, col_acc, col_too,
    col_sum, faults, slow_row, full, sems, point_sem,
):
    source_count, pieces_per, lanes = row_pot.shape
    target_count = col_pot.shape[0]
    block = pieces_per * lanes
    width = points.shape[1]
    own, active = meta[0], meta[1]

    biases = (bias_a, bias_b, bias_c, bias_d)
    row_sides, col_sides = (row_acc, row_too), (col_acc, col_too)
    ring = blocks.shape[0]

    def start_fetch(position):
        slot = lax.rem(position, ring)

        @pl.when(position < own)
        def _():
            start = pl.multiple_of(listed[position] * block, block)
            pltpu.make_async_copy(
                targets.at[pl.ds(start, block), :], blocks.at[slot], sems.at[slot]
            ).start()

        @pl.when((position >= own) & (position < active))
        def _():
            pltpu.make_async_copy(
                foreign.at[position - own], blocks.at[slot], sems.at[slot]
            ).start()

    bring = pltpu.make_async_copy(stored, points, point_sem)
    bring.start()
    for ahead in range(ring - 2):
        start_fetch(jnp.int32(ahead))

    for h in range(pieces_per):
        shifted = row_pot[:, h, :] - row_sq[:, h, :]
        parts = [part.astype(jnp.float32) for part in pieces(shifted)]
        ones = jnp.ones((3, lanes), jnp.float32)
        pad = jnp.zeros((width - 3 * source_count - 3, lanes), jnp.float32)
        turned = jnp.concatenate(parts + [ones, pad], axis=0).T
        features[h * lanes : (h + 1) * lanes, :] = turned.astype(jnp.bfloat16)
    tallest = jnp.maximum(jnp.max(col_pot[...]), jnp.max(far_pot[...]))
    offset = (jnp.max(row_pot[...]) + tallest) / epsilon - headroom
    row_acc[...] = jnp.zeros_like(row_acc)
    row_too[...] = jnp.zeros_like(row_too)
    col_sum[...] = jnp.zeros_like(col_sum)
    faults[...] = jnp.zeros_like(faults)
    lane = lax.broadcasted_iota(jnp.int32, (1, width), 1)

    def pattern(source):
        chosen = (lax.rem(lane, source_count) == source) & (lane < 3 * source_count)
        return jnp.where(chosen, 1.0, 0.0).astype(jnp.bfloat16)

    def prepare(position, which):
        target = listed[jnp.minimum(position, active - 1)]
        near = jnp.minimum(target, target_count - 1)
        far = jnp.maximum(target - target_count, 0)
        term = jnp.where(
            target < target_count, col_pot[near] - col_sq[near], far_pot[far] - far_sq[far]
        )
        parts = [part.astype(jnp.float32) for part in pieces(term - offset * epsilon)]
        before = jnp.zeros((3 * source_count, lanes), jnp.float32)
        after = jnp.zeros((width - 3 * source_count - 3, lanes), jnp.float32)
        for h in range(pieces_per):
            rows = [before] + [part[h : h + 1, :] for part in parts] + [after]
            turned = jnp.concatenate(rows, axis=0).T
            biases[which][h * lanes : (h + 1) * lanes, :] = turned.astype(jnp.bfloat16)

    def right_side(position, which, source, cols):
        extra = biases[which][cols, :] + pattern(source)
        return jnp.concatenate([blocks[lax.rem(position, ring), cols, :], extra], axis=1)

    def fast_tile(position, which, target, source):
        side = which % 2
        rows = pl.ds(pl.multiple_of(source * block, block), block)
        lhs = jnp.concatenate([points[rows, :], features[...]], axis=1)
        for c in range(block // 256):
            cols = slice(c * 256, (c + 1) * 256)
            s = lax.dot_general(
                lhs, right_side(position, which, source, cols), NT,
                preferred_element_type=jnp.float32,
            )
            e = jnp.exp2(s * (log2e / epsilon))
            row_sides[side][rows, :] += e[:, :128] + e[:, 128:]
            col_sides[side][:, cols] += jnp.sum(e.reshape(block // 8, 8, 256), axis=0)

    def fast_end(target, side):
        summed = jnp.sum(col_sides[side][...], axis=0, keepdims=True)
        safe = (summed > smallest) & (summed < largest)
        faults[0:1, :] = jnp.maximum(faults[0:1, :], jnp.where(safe, 0.0, 1.0))
        for h in range(pieces_per):
            col_sum[target, h : h + 1, :] = summed[:, h * lanes : (h + 1) * lanes]

    def lowest_source(mask):
        return bit_count((mask & -mask) - 1)

    def remaining(position, which, target, mask, tile):
        def each(_, left):
            tile(position, which, target, lowest_source(left))
            return left & (left - 1)

        lax.fori_loop(0, bit_count(mask), each, mask)

    def fast_turn(first, near, later):
        second = first + 1
        paired = second < active
        fetch_wait(first)

        @pl.when(paired)
        def _():
            fetch_wait(second)

        start_fetch(first + ring - 2)
        start_fetch(first + ring - 1)
        target = listed[first]
        target_too = listed[jnp.minimum(second, active - 1)]
        mask, mask_too = masks[target], masks[target_too]
        col_acc[...] = jnp.zeros_like(col_acc)
        col_too[...] = jnp.zeros_like(col_too)

        @pl.when(paired)
        def _():
            prepare(first + 2, later)
            prepare(first + 3, later + 1)
            fast_tile(first, near, target, lowest_source(mask))
            fast_tile(second, near + 1, target_too, lowest_source(mask_too))

        rest = jnp.where(paired, mask & (mask - 1), mask)
        remaining(first, near, target, rest, fast_tile)
        fast_end(target, 0)

        @pl.when(paired)
        def _():
            remaining(second, near + 1, target_too, mask_too & (mask_too - 1), fast_tile)
            fast_end(target_too, 1)

    def slow_tile(position, which, target, source):
        first_row = pl.multiple_of(source * block, block)
        full[8:16, :] = jnp.full((8, block), absent, jnp.float32)

        def logits(r):
            rows = pl.ds(pl.multiple_of(first_row + r * 128, 128), 128)
            near = pl.ds(pl.multiple_of(r * 128, 128), 128)
            lhs = jnp.concatenate([points[rows, :], features[near, :]], axis=1)
            made = []
            for c in range(block // 256):
                rhs = right_side(position, which, source, slice(c * 256, (c + 1) * 256))
                made.append(lax.dot_general(lhs, rhs, NT, preferred_element_type=jnp.float32))
            return rows, jnp.concatenate(made, axis=1) * (1.0 / epsilon)

        def first_pass(r, carry):
            rows, t = logits(r)
            top = jnp.max(t, axis=1, keepdims=True)
            lse = top + jnp.log(jnp.sum(jnp.exp(t - top), axis=1, keepdims=True))
            slow_row[rows, :] = log_add(slow_row[rows, :], jnp.broadcast_to(lse, (128, width)))
            full[8:9, :] = jnp.maximum(full[8:9, :], jnp.max(t, axis=0, keepdims=True))
            return carry

        lax.fori_loop(0, block // 128, first_pass, 0)
        full[16:17, :] = jnp.zeros((1, block), jnp.float32)

        def second_pass(r, carry):
            rows, t = logits(r)
            full[16:17, :] += jnp.sum(jnp.exp(t - full[8:9, :]), axis=0, keepdims=True)
            return carry

        lax.fori_loop(0, block // 128, second_pass, 0)
        lse = full[8:9, :] + jnp.log(full[16:17, :])
        col_acc[0:1, :] = log_add(col_acc[0:1, :], lse)

    def slow_end(target):
        for h in range(pieces_per):
            col_sum[target, h : h + 1, :] = col_acc[0:1, h * lanes : (h + 1) * lanes]

    def slow_visit(position, carry):
        target = listed[position]
        fetch_wait(position)
        start_fetch(position + ring - 2)
        prepare(position, 0)
        col_acc[...] = jnp.full(col_acc.shape, absent, jnp.float32)
        remaining(position, 0, target, masks[target], slow_tile)
        slow_end(target)
        return carry

    def four_blocks(turn, carry):
        fast_turn(4 * turn, 0, 2)

        @pl.when(4 * turn + 2 < active)
        def _():
            fast_turn(4 * turn + 2, 2, 0)

        return carry

    def fetch_wait(position):
        slot = lax.rem(position, ring)
        pltpu.make_async_copy(
            targets.at[pl.ds(0, block), :], blocks.at[slot], sems.at[slot]
        ).wait()

    bring.wait()

    @pl.when(active > 0)
    def _():
        prepare(0, 0)
        prepare(1, 1)

    lax.fori_loop(0, (active + 3) // 4, four_blocks, 0)

    def put_rows(source, row):
        for h in range(pieces_per):
            row_out[source, h : h + 1, :] = row[:, h * lanes : (h + 1) * lanes]

    for source in range(source_count):
        first_row = source * block
        summed = jnp.concatenate(
            [
                lane_sums(row_acc[rows, :] + row_too[rows, :])
                for rows in (
                    slice(first_row + h * lanes, first_row + (h + 1) * lanes)
                    for h in range(pieces_per)
                )
            ],
            axis=1,
        )
        wanted = ((meta[2] >> source) & 1) == 1
        safe = ((summed > smallest) & (summed < largest)) | jnp.logical_not(wanted)
        faults[0:1, :] = jnp.maximum(faults[0:1, :], jnp.where(safe, 0.0, 1.0))
        put_rows(source, jnp.where(summed > 0, jnp.log(summed) + offset, absent))
    sums = col_sum[...]
    made = jnp.where(sums > 0, jnp.log(sums) + offset, absent)
    col_out[...] = made[:target_count]
    far_out[...] = made[target_count:]

    @pl.when(jnp.max(faults[0:1, :]) > 0)
    def _():
        slow_row[...] = jnp.full(slow_row.shape, absent, jnp.float32)
        col_sum[...] = jnp.full(col_sum.shape, absent, jnp.float32)
        for ahead in range(ring - 2):
            start_fetch(jnp.int32(ahead))
        lax.fori_loop(0, active, slow_visit, 0)
        col_out[...] = col_sum[:target_count] + offset
        far_out[...] = col_sum[target_count:] + offset
        for source in range(source_count):
            put_rows(source, lane_first(slow_row[source * block : (source + 1) * block, :]) + offset)


def sweep(masks, listed, meta, points, targets, foreign, *cells):
    row_pot, col_pot = cells[0], cells[2]
    source_count, pieces_per, lanes = row_pot.shape
    target_count = col_pot.shape[0]
    block = pieces_per * lanes
    width = points.shape[1]
    vmem = pl.BlockSpec(memory_space=pltpu.VMEM)
    smem = pl.BlockSpec(memory_space=pltpu.SMEM)
    anywhere = pl.BlockSpec(memory_space=pl.ANY)
    rows = jax.ShapeDtypeStruct(row_pot.shape, jnp.float32)
    cols = jax.ShapeDtypeStruct(col_pot.shape, jnp.float32)
    pairs = 3 * source_count
    return pl.pallas_call(
        sweep_kernel,
        out_shape=(rows, cols, cols),
        in_specs=[smem, smem, smem, anywhere, anywhere, anywhere] + [vmem] * len(cells),
        out_specs=(vmem, vmem, vmem),
        scratch_shapes=[
            pltpu.VMEM(points.shape, points.dtype),
            pltpu.VMEM((6, block, width), jnp.bfloat16),
            pltpu.VMEM((block, width), jnp.bfloat16),
            pltpu.VMEM((block, width), jnp.bfloat16),
            pltpu.VMEM((block, width), jnp.bfloat16),
            pltpu.VMEM((block, width), jnp.bfloat16),
            pltpu.VMEM((block, width), jnp.bfloat16),
            pltpu.VMEM((source_count * block, width), jnp.float32),
            pltpu.VMEM((source_count * block, width), jnp.float32),
            pltpu.VMEM((8, block), jnp.float32),
            pltpu.VMEM((8, block), jnp.float32),
            pltpu.VMEM((2 * target_count, pieces_per, lanes), jnp.float32),
            pltpu.VMEM((8, block), jnp.float32),
            pltpu.VMEM((source_count * block, width), jnp.float32),
            pltpu.VMEM((24, block), jnp.float32),
            pltpu.SemaphoreType.DMA((6,)),
            pltpu.SemaphoreType.DMA,
        ],
        compiler_params=pltpu.CompilerParams(vmem_limit_bytes=40 * 1024 * 1024),
        cost_estimate=pl.CostEstimate(
            flops=2 * pairs * block * block * width,
            bytes_accessed=pairs * block * width * 2,
            transcendentals=pairs * block * block,
        ),
        name="sweep",
    )(masks, listed, meta, points, targets, foreign, *cells)


def swapped(value, axis, size, step):
    return lax.ppermute(value, axis, [(i, i ^ step) for i in range(size)])


def exchange(value, axis, size, other_axis, other_size):
    steps = []
    while 2 ** len(steps) < size:
        steps.append(2 ** len(steps))
    if not steps:
        return value
    orders = [steps, steps[1:] + steps[:1]]

    def swap(sent, turn):
        pairs = [
            (i * other_size + k, (i ^ orders[k % 2][turn]) * other_size + k)
            for i in range(size)
            for k in range(other_size)
        ]
        return lax.ppermute(sent, (axis, other_axis), pairs)

    half = value.shape[0] // 2
    odd = lax.rem(lax.axis_index(other_axis), 2) == 1
    me = lax.axis_index(axis)
    low = jnp.where(odd, lax.rem(me // orders[1][0], 2), lax.rem(me // orders[0][0], 2))
    kept = lax.dynamic_slice_in_dim(value, low * half, half, 0)
    sent = lax.dynamic_slice_in_dim(value, (1 - low) * half, half, 0)
    kept = log_add(kept, swap(sent, 0))
    for turn in range(1, len(steps)):
        kept = log_add(kept, swap(kept, turn))
    other = swap(kept, 0)
    first = low == 0
    return jnp.concatenate([jnp.where(first, kept, other), jnp.where(first, other, kept)], axis=0)


def doubled(value, axis, size):
    step = 1
    while step < size:
        value = log_add(value, swapped(value, axis, size, step))
        step *= 2
    return value


def local(
    source_points, target_points, source_potential, target_potential,
    source_log_mass, target_log_mass, pair_targets, pair_counts,
):
    source_count = pair_targets.shape[0]
    block = source_points.shape[0] // source_count
    src_size, tgt_size = lax.axis_size("src"), lax.axis_size("tgt")
    rank = lax.axis_index("tgt").astype(jnp.int32).reshape(1)

    def by_block(value):
        return value.reshape(-1, block // 128, 128)

    masks, listed, meta, named_blocks, packed = plan(pair_targets, pair_counts, rank, target_points, block)
    foreign = swapped(packed, "tgt", tgt_size, 1)
    row_pot, col_pot = by_block(source_potential), by_block(target_potential)
    row_mass, col_mass = by_block(source_log_mass), by_block(target_log_mass)
    row_sq = by_block(half_squares(source_points))
    col_sq = named_squares(meta, named_blocks, target_points, block)
    far_sq = swapped(col_sq, "tgt", tgt_size, 1)
    for _ in range(ITERS):
        far_pot = swapped(col_pot, "tgt", tgt_size, 1)
        rows, cols, far = sweep(
            masks, listed, meta, source_points, target_points, foreign,
            row_pot, row_sq, col_pot, col_sq, far_pot, far_sq,
        )
        cols = log_add(cols, swapped(far, "tgt", tgt_size, 1))
        rows = doubled(rows, "tgt", tgt_size)
        cols = exchange(cols, "src", src_size, "tgt", tgt_size)
        row_pot = row_pot + (0.5 * epsilon) * (row_mass - rows)
        col_pot = col_pot + (0.5 * epsilon) * (col_mass - cols)
    return row_pot.reshape(-1), col_pot.reshape(-1)


def solution(mesh):
    placed = (
        P("src", None), P("tgt", None), P("src"), P("tgt"),
        P("src"), P("tgt"), P("src", None), P("src"),
    )
    return jax.shard_map(
        local, mesh=mesh, in_specs=placed, out_specs=(P("src"), P("tgt")), check_vma=False
    )
```

```python
import functools
import jax
import jax.numpy as jnp
from jax import lax
from jax.experimental import pallas as pl
from jax.experimental.pallas import tpu as pltpu
from jax.sharding import PartitionSpec as P

ITERS = 2
moved_cap = 8
epsilon = 0.5
absent = -1e30
log2e = 1.4426950408889634
headroom = 60.0
smallest = 1e-26
largest = 1e37
NT = (((1,), (1,)), ((), ()))


def pieces(value):
    high = value.astype(jnp.bfloat16)
    rest = value - high.astype(jnp.float32)
    middle = rest.astype(jnp.bfloat16)
    low = (rest - middle.astype(jnp.float32)).astype(jnp.bfloat16)
    return high, middle, low


def lane_sums(block):
    return jnp.sum(block.T, axis=0, keepdims=True)


def two_pieces(value):
    high = value.astype(jnp.bfloat16)
    low = (value - high.astype(jnp.float32)).astype(jnp.bfloat16)
    return jnp.concatenate([high, low], axis=1)


def lane_first(block):
    lane = lax.broadcasted_iota(jnp.int32, (8, block.shape[1]), 1)
    pick = jnp.where(lane == 0, 1.0, 0.0).astype(jnp.bfloat16)
    total = None
    for part in pieces(block):
        product = lax.dot_general(pick, part, NT, preferred_element_type=jnp.float32)
        total = product if total is None else total + product
    return total[0:1]


def log_add(first, second):
    top = jnp.maximum(first, second)
    return top + jnp.log(jnp.exp(first - top) + jnp.exp(second - top))


def bit_count(value):
    value = value - ((value >> 1) & 0x55555555)
    value = (value & 0x33333333) + ((value >> 2) & 0x33333333)
    value = (value + (value >> 4)) & 0x0F0F0F0F
    return (value * 0x01010101) >> 24


def plan_kernel(
    pair_targets, pair_counts, rank, targets,
    masks, listed, meta, named_blocks, packed,
    both, slots, state, several, single, staged, sems, out_sems,
):
    source_count, slot_width = pair_targets.shape
    total = both.shape[0] - 1
    target_count = total // 2
    block = packed.shape[1]
    mine = lax.rem(rank[0], 2)
    base = (rank[0] - mine) * target_count
    for index in range(total + 1):
        both[index] = 0
    low_load = jnp.int32(0)
    high_load = jnp.int32(0)
    for source in range(source_count):
        count = pair_counts[source]
        for slot in range(slot_width):
            place = pair_targets[source, slot] - base
            here = (slot < count) & (place >= 0) & (place < total)
            index = jnp.where(here, place, total)
            both[index] = both[index] | (1 << source)
            low_load = low_load + jnp.where(here & (place < target_count), 1, 0)
            high_load = high_load + jnp.where(here & (place >= target_count), 1, 0)
    named = jnp.int32(0)
    for index in range(target_count):
        named_blocks[named] = index
        named = named + jnp.where(both[mine * target_count + index] != 0, 1, 0)
    meta[3] = named
    heavy = jnp.where(high_load > low_load, 1, 0)
    wanted = jnp.abs(high_load - low_load) // 2
    state[0] = 0
    state[1] = 0
    first = heavy * target_count
    giving = mine == heavy

    several_count = jnp.int32(0)
    single_count = jnp.int32(0)
    for index in range(target_count):
        mask = both[first + index]
        more = (mask & (mask - 1)) != 0
        several[several_count] = index
        single[single_count] = index
        several_count = several_count + jnp.where(more, 1, 0)
        single_count = single_count + jnp.where((mask != 0) & jnp.logical_not(more), 1, 0)

    def move(index, mask, count):
        place = state[0]
        state[0] = place + 1
        state[1] = state[1] + count

        @pl.when(giving)
        def _():
            both[first + index] = 0
            start = pl.multiple_of(index * block, block)
            pltpu.make_async_copy(
                targets.at[pl.ds(start, block), :], staged.at[place], sems.at[place]
            ).start()

        @pl.when(jnp.logical_not(giving))
        def _():
            slots[place] = target_count + index
            masks[target_count + index] = mask

    def offer_several(at, carry):
        index = several[at]
        mask = both[first + index]
        count = bit_count(mask)

        @pl.when((state[0] < packed.shape[0]) & (state[1] + count <= wanted))
        def _():
            move(index, mask, count)

        return carry

    def offer_single(at, carry):
        index = single[at]
        move(index, both[first + index], 1)
        return carry

    lax.fori_loop(0, several_count, offer_several, 0)
    room = jnp.minimum(packed.shape[0] - state[0], wanted - state[1])
    lax.fori_loop(0, jnp.minimum(single_count, room), offer_single, 0)
    count = jnp.int32(0)
    union = jnp.int32(0)
    for index in range(target_count):
        mask = both[mine * target_count + index]
        masks[index] = mask
        listed[count] = index
        count = count + jnp.where(mask != 0, 1, 0)
        union = union | mask
    own = count
    foreign = jnp.where(giving, 0, state[0])

    def append(place, gathered):
        index = slots[place]
        listed[own + place] = index
        return gathered | masks[index]

    union = lax.fori_loop(0, foreign, append, union)
    meta[0] = own
    meta[1] = own + foreign
    meta[2] = union

    def put_out(place):
        return pltpu.make_async_copy(staged.at[place], packed.at[place], out_sems.at[place])

    def pass_on(place, carry):
        pltpu.make_async_copy(
            targets.at[pl.ds(0, block), :], staged.at[place], sems.at[place]
        ).wait()
        put_out(place).start()
        return carry

    def finish(place, carry):
        put_out(place).wait()
        return carry

    sent = jnp.where(giving, state[0], 0)
    lax.fori_loop(0, sent, pass_on, 0)
    lax.fori_loop(0, sent, finish, 0)


def plan(pair_targets, pair_counts, rank, targets, block):
    total = 2 * (targets.shape[0] // block)
    cap = min(moved_cap, total // 2)
    smem = pl.BlockSpec(memory_space=pltpu.SMEM)
    table = jax.ShapeDtypeStruct((total + 1,), jnp.int32)
    return pl.pallas_call(
        plan_kernel,
        out_shape=(
            table, table, jax.ShapeDtypeStruct((8,), jnp.int32), table,
            jax.ShapeDtypeStruct((cap, block, targets.shape[1]), targets.dtype),
        ),
        in_specs=[smem, smem, smem, pl.BlockSpec(memory_space=pl.ANY)],
        out_specs=(smem, smem, smem, smem, pl.BlockSpec(memory_space=pl.ANY)),
        scratch_shapes=[
            pltpu.SMEM((total + 1,), jnp.int32),
            pltpu.SMEM((cap,), jnp.int32),
            pltpu.SMEM((2,), jnp.int32),
            pltpu.SMEM((total + 1,), jnp.int32),
            pltpu.SMEM((total + 1,), jnp.int32),
            pltpu.VMEM((cap, block, targets.shape[1]), targets.dtype),
            pltpu.SemaphoreType.DMA((cap,)),
            pltpu.SemaphoreType.DMA((cap,)),
        ],
        name="plan",
    )(pair_targets, pair_counts, rank, targets)


def squares_kernel(meta, named_blocks, points, out, buffer, sums, sems):
    pieces_per, lanes = out.shape[1:]
    block = pieces_per * lanes
    slots = buffer.shape[0]
    ones = jnp.ones((8, 2 * points.shape[1]), jnp.bfloat16)
    count = meta[3]

    def fetch(position):
        slot = lax.rem(position, slots)
        start = pl.multiple_of(named_blocks[position] * block, block)
        return pltpu.make_async_copy(
            points.at[pl.ds(start, block), :], buffer.at[slot], sems.at[slot]
        )

    def begin(position):
        @pl.when(position < count)
        def _():
            fetch(position).start()

    group = sums.shape[0]
    for position in range(slots - group):
        begin(jnp.int32(position))
    out[...] = jnp.zeros_like(out)

    def visit(turn, carry):
        first = turn * group
        for at in range(group):
            begin(first + slots - group + at)
        for at in range(group):
            @pl.when(first + at < count)
            def _():
                fetch(first + at).wait()
        side = lax.rem(first, slots)
        for at in range(group):
            wide = buffer[side + at].astype(jnp.float32)
            square = wide * wide
            if at % 2 == 0:
                summed = lax.dot_general(
                    ones, two_pieces(square), NT, preferred_element_type=jnp.float32
                )
            for h in range(pieces_per):
                part = slice(h * lanes, (h + 1) * lanes)
                row = summed[0:1, part] if at % 2 == 0 else lane_sums(square[part, :])
                sums[at, h : h + 1, :] = 0.5 * row
        for at in range(group):
            @pl.when(first + at < count)
            def _():
                out[named_blocks[first + at]] = sums[at]
        return carry

    lax.fori_loop(0, (count + group - 1) // group, visit, 0)


def named_squares(meta, named_blocks, points, block):
    smem = pl.BlockSpec(memory_space=pltpu.SMEM)
    return pl.pallas_call(
        squares_kernel,
        out_shape=jax.ShapeDtypeStruct((points.shape[0] // block, block // 128, 128), jnp.float32),
        in_specs=[smem, smem, pl.BlockSpec(memory_space=pl.ANY)],
        out_specs=pl.BlockSpec(memory_space=pltpu.VMEM),
        scratch_shapes=[
            pltpu.VMEM((16, block, points.shape[1]), points.dtype),
            pltpu.VMEM((4, block // 128, 128), jnp.float32),
            pltpu.SemaphoreType.DMA((16,)),
        ],
        cost_estimate=pl.CostEstimate(
            flops=2 * points.size, bytes_accessed=2 * points.size, transcendentals=0
        ),
        name="squares",
    )(meta, named_blocks, points)


def half_squares(points):
    widened = points.astype(jnp.float32)
    return 0.5 * jnp.sum(widened * widened, axis=1)


def sweep_kernel(
    masks, listed, meta, stored, targets, foreign,
    row_pot, row_sq, col_pot, col_sq, far_pot, far_sq,
    row_out, col_out, far_out,
    points, blocks, bias_a, bias_b, bias_c, bias_d, features, row_acc, col_acc, col_too,
    col_sum, faults, slow_row, full, sems, point_sem,
):
    source_count, pieces_per, lanes = row_pot.shape
    target_count = col_pot.shape[0]
    block = pieces_per * lanes
    width = points.shape[1]
    own, active = meta[0], meta[1]

    biases = (bias_a, bias_b, bias_c, bias_d)
    col_sides = (col_acc, col_too)
    ring = blocks.shape[0]

    def start_fetch(position):
        slot = lax.rem(position, ring)

        @pl.when(position < own)
        def _():
            start = pl.multiple_of(listed[position] * block, block)
            pltpu.make_async_copy(
                targets.at[pl.ds(start, block), :], blocks.at[slot], sems.at[slot]
            ).start()

        @pl.when((position >= own) & (position < active))
        def _():
            pltpu.make_async_copy(
                foreign.at[position - own], blocks.at[slot], sems.at[slot]
            ).start()

    bring = pltpu.make_async_copy(stored, points, point_sem)
    bring.start()
    for ahead in range(ring - 2):
        start_fetch(jnp.int32(ahead))

    for h in range(pieces_per):
        shifted = row_pot[:, h, :] - row_sq[:, h, :]
        parts = [part.astype(jnp.float32) for part in pieces(shifted)]
        ones = jnp.ones((3, lanes), jnp.float32)
        pad = jnp.zeros((width - 3 * source_count - 3, lanes), jnp.float32)
        turned = jnp.concatenate(parts + [ones, pad], axis=0).T
        features[h * lanes : (h + 1) * lanes, :] = turned.astype(jnp.bfloat16)
    tallest = jnp.maximum(jnp.max(col_pot[...]), jnp.max(far_pot[...]))
    offset = (jnp.max(row_pot[...]) + tallest) / epsilon - headroom
    row_acc[...] = jnp.zeros_like(row_acc)
    col_sum[...] = jnp.zeros_like(col_sum)
    faults[...] = jnp.zeros_like(faults)
    lane = lax.broadcasted_iota(jnp.int32, (1, width), 1)

    def pattern(source):
        chosen = (lax.rem(lane, source_count) == source) & (lane < 3 * source_count)
        return jnp.where(chosen, 1.0, 0.0).astype(jnp.bfloat16)

    def prepare(position, which):
        target = listed[jnp.minimum(position, active - 1)]
        near = jnp.minimum(target, target_count - 1)
        far = jnp.maximum(target - target_count, 0)
        term = jnp.where(
            target < target_count, col_pot[near] - col_sq[near], far_pot[far] - far_sq[far]
        )
        parts = [part.astype(jnp.float32) for part in pieces(term - offset * epsilon)]
        before = jnp.zeros((3 * source_count, lanes), jnp.float32)
        after = jnp.zeros((width - 3 * source_count - 3, lanes), jnp.float32)
        for h in range(pieces_per):
            rows = [before] + [part[h : h + 1, :] for part in parts] + [after]
            turned = jnp.concatenate(rows, axis=0).T
            biases[which][h * lanes : (h + 1) * lanes, :] = turned.astype(jnp.bfloat16)

    def right_side(position, which, source, cols):
        extra = biases[which][cols, :] + pattern(source)
        return jnp.concatenate([blocks[lax.rem(position, ring), cols, :], extra], axis=1)

    def fast_tile(position, which, target, source):
        side = which % 2
        rows = pl.ds(pl.multiple_of(source * block, block), block)
        lhs = jnp.concatenate([points[rows, :], features[...]], axis=1)
        for c in range(block // 256):
            cols = slice(c * 256, (c + 1) * 256)
            s = lax.dot_general(
                lhs, right_side(position, which, source, cols), NT,
                preferred_element_type=jnp.float32,
            )
            e = jnp.exp2(s * (log2e / epsilon))
            row_acc[rows, :] += e[:, :128] + e[:, 128:]
            col_sides[side][:, cols] += jnp.sum(e.reshape(block // 8, 8, 256), axis=0)

    def fast_end(target, side):
        summed = jnp.sum(col_sides[side][...], axis=0, keepdims=True)
        safe = (summed > smallest) & (summed < largest)
        faults[0:1, :] = jnp.maximum(faults[0:1, :], jnp.where(safe, 0.0, 1.0))
        for h in range(pieces_per):
            col_sum[target, h : h + 1, :] = summed[:, h * lanes : (h + 1) * lanes]

    def lowest_source(mask):
        return bit_count((mask & -mask) - 1)

    def remaining(position, which, target, mask, tile):
        def each(_, left):
            tile(position, which, target, lowest_source(left))
            return left & (left - 1)

        lax.fori_loop(0, bit_count(mask), each, mask)

    def fast_turn(first, near, later):
        second = first + 1
        paired = second < active
        fetch_wait(first)

        @pl.when(paired)
        def _():
            fetch_wait(second)

        start_fetch(first + ring - 2)
        start_fetch(first + ring - 1)
        target = listed[first]
        target_too = listed[jnp.minimum(second, active - 1)]
        mask, mask_too = masks[target], masks[target_too]
        col_acc[...] = jnp.zeros_like(col_acc)
        col_too[...] = jnp.zeros_like(col_too)

        @pl.when(paired)
        def _():
            prepare(first + 2, later)
            prepare(first + 3, later + 1)
            fast_tile(first, near, target, lowest_source(mask))
            fast_tile(second, near + 1, target_too, lowest_source(mask_too))

        rest = jnp.where(paired, mask & (mask - 1), mask)
        remaining(first, near, target, rest, fast_tile)
        fast_end(target, 0)

        @pl.when(paired)
        def _():
            remaining(second, near + 1, target_too, mask_too & (mask_too - 1), fast_tile)
            fast_end(target_too, 1)

    def slow_tile(position, which, target, source):
        first_row = pl.multiple_of(source * block, block)
        full[8:16, :] = jnp.full((8, block), absent, jnp.float32)

        def logits(r):
            rows = pl.ds(pl.multiple_of(first_row + r * 128, 128), 128)
            near = pl.ds(pl.multiple_of(r * 128, 128), 128)
            lhs = jnp.concatenate([points[rows, :], features[near, :]], axis=1)
            made = []
            for c in range(block // 256):
                rhs = right_side(position, which, source, slice(c * 256, (c + 1) * 256))
                made.append(lax.dot_general(lhs, rhs, NT, preferred_element_type=jnp.float32))
            return rows, jnp.concatenate(made, axis=1) * (1.0 / epsilon)

        def first_pass(r, carry):
            rows, t = logits(r)
            top = jnp.max(t, axis=1, keepdims=True)
            lse = top + jnp.log(jnp.sum(jnp.exp(t - top), axis=1, keepdims=True))
            slow_row[rows, :] = log_add(slow_row[rows, :], jnp.broadcast_to(lse, (128, width)))
            full[8:9, :] = jnp.maximum(full[8:9, :], jnp.max(t, axis=0, keepdims=True))
            return carry

        lax.fori_loop(0, block // 128, first_pass, 0)
        full[16:17, :] = jnp.zeros((1, block), jnp.float32)

        def second_pass(r, carry):
            rows, t = logits(r)
            full[16:17, :] += jnp.sum(jnp.exp(t - full[8:9, :]), axis=0, keepdims=True)
            return carry

        lax.fori_loop(0, block // 128, second_pass, 0)
        lse = full[8:9, :] + jnp.log(full[16:17, :])
        col_acc[0:1, :] = log_add(col_acc[0:1, :], lse)

    def slow_end(target):
        for h in range(pieces_per):
            col_sum[target, h : h + 1, :] = col_acc[0:1, h * lanes : (h + 1) * lanes]

    def slow_visit(position, carry):
        target = listed[position]
        fetch_wait(position)
        start_fetch(position + ring - 2)
        prepare(position, 0)
        col_acc[...] = jnp.full(col_acc.shape, absent, jnp.float32)
        remaining(position, 0, target, masks[target], slow_tile)
        slow_end(target)
        return carry

    def four_blocks(turn, carry):
        fast_turn(4 * turn, 0, 2)

        @pl.when(4 * turn + 2 < active)
        def _():
            fast_turn(4 * turn + 2, 2, 0)

        return carry

    def fetch_wait(position):
        slot = lax.rem(position, ring)
        pltpu.make_async_copy(
            targets.at[pl.ds(0, block), :], blocks.at[slot], sems.at[slot]
        ).wait()

    bring.wait()

    @pl.when(active > 0)
    def _():
        prepare(0, 0)
        prepare(1, 1)

    lax.fori_loop(0, (active + 3) // 4, four_blocks, 0)

    def put_rows(source, row):
        for h in range(pieces_per):
            row_out[source, h : h + 1, :] = row[:, h * lanes : (h + 1) * lanes]

    for source in range(source_count):
        first_row = source * block
        if source % 2 == 0:
            ones = jnp.ones((8, 2 * width), jnp.bfloat16)
            pair = two_pieces(row_acc[first_row : first_row + block, :])
            summed = lax.dot_general(ones, pair, NT, preferred_element_type=jnp.float32)[0:1]
        else:
            summed = jnp.concatenate(
                [
                    lane_sums(row_acc[first_row + h * lanes : first_row + (h + 1) * lanes, :])
                    for h in range(pieces_per)
                ],
                axis=1,
            )
        wanted = ((meta[2] >> source) & 1) == 1
        safe = ((summed > smallest) & (summed < largest)) | jnp.logical_not(wanted)
        faults[0:1, :] = jnp.maximum(faults[0:1, :], jnp.where(safe, 0.0, 1.0))
        put_rows(source, jnp.where(summed > 0, jnp.log(summed) + offset, absent))
    sums = col_sum[...]
    made = jnp.where(sums > 0, jnp.log(sums) + offset, absent)
    col_out[...] = made[:target_count]
    far_out[...] = made[target_count:]

    @pl.when(jnp.max(faults[0:1, :]) > 0)
    def _():
        slow_row[...] = jnp.full(slow_row.shape, absent, jnp.float32)
        col_sum[...] = jnp.full(col_sum.shape, absent, jnp.float32)
        for ahead in range(ring - 2):
            start_fetch(jnp.int32(ahead))
        lax.fori_loop(0, active, slow_visit, 0)
        col_out[...] = col_sum[:target_count] + offset
        far_out[...] = col_sum[target_count:] + offset
        for source in range(source_count):
            put_rows(source, lane_first(slow_row[source * block : (source + 1) * block, :]) + offset)


def sweep(masks, listed, meta, points, targets, foreign, *cells):
    row_pot, col_pot = cells[0], cells[2]
    source_count, pieces_per, lanes = row_pot.shape
    target_count = col_pot.shape[0]
    block = pieces_per * lanes
    width = points.shape[1]
    vmem = pl.BlockSpec(memory_space=pltpu.VMEM)
    smem = pl.BlockSpec(memory_space=pltpu.SMEM)
    anywhere = pl.BlockSpec(memory_space=pl.ANY)
    rows = jax.ShapeDtypeStruct(row_pot.shape, jnp.float32)
    cols = jax.ShapeDtypeStruct(col_pot.shape, jnp.float32)
    pairs = 3 * source_count
    return pl.pallas_call(
        sweep_kernel,
        out_shape=(rows, cols, cols),
        in_specs=[smem, smem, smem, anywhere, anywhere, anywhere] + [vmem] * len(cells),
        out_specs=(vmem, vmem, vmem),
        scratch_shapes=[
            pltpu.VMEM(points.shape, points.dtype),
            pltpu.VMEM((6, block, width), jnp.bfloat16),
            pltpu.VMEM((block, width), jnp.bfloat16),
            pltpu.VMEM((block, width), jnp.bfloat16),
            pltpu.VMEM((block, width), jnp.bfloat16),
            pltpu.VMEM((block, width), jnp.bfloat16),
            pltpu.VMEM((block, width), jnp.bfloat16),
            pltpu.VMEM((source_count * block, width), jnp.float32),
            pltpu.VMEM((8, block), jnp.float32),
            pltpu.VMEM((8, block), jnp.float32),
            pltpu.VMEM((2 * target_count, pieces_per, lanes), jnp.float32),
            pltpu.VMEM((8, block), jnp.float32),
            pltpu.VMEM((source_count * block, width), jnp.float32),
            pltpu.VMEM((24, block), jnp.float32),
            pltpu.SemaphoreType.DMA((6,)),
            pltpu.SemaphoreType.DMA,
        ],
        compiler_params=pltpu.CompilerParams(vmem_limit_bytes=40 * 1024 * 1024),
        cost_estimate=pl.CostEstimate(
            flops=2 * pairs * block * block * width,
            bytes_accessed=pairs * block * width * 2,
            transcendentals=pairs * block * block,
        ),
        name="sweep",
    )(masks, listed, meta, points, targets, foreign, *cells)


def swapped(value, axis, size, step):
    return lax.ppermute(value, axis, [(i, i ^ step) for i in range(size)])


def exchange(value, axis, size, other_axis, other_size):
    steps = []
    while 2 ** len(steps) < size:
        steps.append(2 ** len(steps))
    if not steps:
        return value
    orders = [steps, steps[1:] + steps[:1]]

    def swap(sent, turn):
        pairs = [
            (i * other_size + k, (i ^ orders[k % 2][turn]) * other_size + k)
            for i in range(size)
            for k in range(other_size)
        ]
        return lax.ppermute(sent, (axis, other_axis), pairs)

    half = value.shape[0] // 2
    odd = lax.rem(lax.axis_index(other_axis), 2) == 1
    me = lax.axis_index(axis)
    low = jnp.where(odd, lax.rem(me // orders[1][0], 2), lax.rem(me // orders[0][0], 2))
    kept = lax.dynamic_slice_in_dim(value, low * half, half, 0)
    sent = lax.dynamic_slice_in_dim(value, (1 - low) * half, half, 0)
    kept = log_add(kept, swap(sent, 0))
    for turn in range(1, len(steps)):
        kept = log_add(kept, swap(kept, turn))
    other = swap(kept, 0)
    first = low == 0
    return jnp.concatenate([jnp.where(first, kept, other), jnp.where(first, other, kept)], axis=0)


def doubled(value, axis, size):
    step = 1
    while step < size:
        value = log_add(value, swapped(value, axis, size, step))
        step *= 2
    return value


def local(
    source_points, target_points, source_potential, target_potential,
    source_log_mass, target_log_mass, pair_targets, pair_counts,
):
    source_count = pair_targets.shape[0]
    block = source_points.shape[0] // source_count
    src_size, tgt_size = lax.axis_size("src"), lax.axis_size("tgt")
    rank = lax.axis_index("tgt").astype(jnp.int32).reshape(1)

    def by_block(value):
        return value.reshape(-1, block // 128, 128)

    masks, listed, meta, named_blocks, packed = plan(pair_targets, pair_counts, rank, target_points, block)
    foreign = swapped(packed, "tgt", tgt_size, 1)
    row_pot, col_pot = by_block(source_potential), by_block(target_potential)
    row_mass, col_mass = by_block(source_log_mass), by_block(target_log_mass)
    row_sq = by_block(half_squares(source_points))
    col_sq = named_squares(meta, named_blocks, target_points, block)
    far_sq = swapped(col_sq, "tgt", tgt_size, 1)
    for _ in range(ITERS):
        far_pot = swapped(col_pot, "tgt", tgt_size, 1)
        rows, cols, far = sweep(
            masks, listed, meta, source_points, target_points, foreign,
            row_pot, row_sq, col_pot, col_sq, far_pot, far_sq,
        )
        cols = log_add(cols, swapped(far, "tgt", tgt_size, 1))
        rows = doubled(rows, "tgt", tgt_size)
        cols = exchange(cols, "src", src_size, "tgt", tgt_size)
        row_pot = row_pot + (0.5 * epsilon) * (row_mass - rows)
        col_pot = col_pot + (0.5 * epsilon) * (col_mass - cols)
    return row_pot.reshape(-1), col_pot.reshape(-1)


def solution(mesh):
    placed = (
        P("src", None), P("tgt", None), P("src"), P("tgt"),
        P("src"), P("tgt"), P("src", None), P("src"),
    )
    return jax.shard_map(
        local, mesh=mesh, in_specs=placed, out_specs=(P("src"), P("tgt")), check_vma=False
    )
```
